512 devices in a mesh: chan: 128 (over y, x_lo, z), pix: 4 (over x_hi, core).
Axes of the slice: x: 4 (x_hi: 2, x_lo: 2; x = x_hi * 2 + x_lo), y: 8, z: 8, core: 2. Of those that a mesh axis runs over, the one named last changes fastest.
Arguments:
- voltages: bfloat16 [256, 2048, 256], P('chan', 'pix'), may hold values from -6 to 6
- fir_taps: float32 [4, 128], replicated, may hold values from -3 to 3
- station_of_slot: int32 [256], replicated, may hold values from 0 to 255, each once
- station_u: int32 [256], replicated, may hold values from 0 to 1023
- station_v: int32 [256], replicated, may hold values from 0 to 1023
- pixel_l: int32 [64], replicated, may hold values from -512 to 511
- pixel_m: int32 [64], replicated, may hold values from -512 to 511
Outputs:
- visibilities: float32 [128, 2, 256, 256], P('chan', None, 'pix')
- image: float32 [128, 4096], P('chan', 'pix')
The draws below stay inside these ranges and needn't reach their ends.
Inputs may be any that keep to these rules, and one draw needn't show every extreme that they name: `station_of_slot`: each station number stands in exactly one slot.
All inputs are finite; a program needn't handle non-finite values.
Results may differ from the reference program's by a relative error of at most 0.012.
Values may be sent and summed in bfloat16 or wider, within the bound.
No kernel may reach another device: no remote copies, remote signals or barrier semaphores. Data moves between devices by JAX's collectives and lax.ppermute only.
A program may use at most 64 MiB of HBM per device.

```python
import math
import jax
import jax.numpy as jnp
from jax import lax

STATIONS = 256
POINTS = 128
TAPS = 4
GRID = 1024
PIX_L = 64
PIX_M = 64
SPECTRA = 2048


def with_ends(array, rng, least, top_value):
    index_at = [jax.random.randint(jax.random.fold_in(rng, axis), (), 0, length) for axis, length in enumerate(array.shape)]
    widest = array.shape.index(max(array.shape))
    beside = index_at[:widest] + [(index_at[widest] + 1) % array.shape[widest]] + index_at[widest + 1:]
    return array.at[tuple(index_at)].set(least).at[tuple(beside)].set(top_value)


def levels(key, shape, split, least, high):
    factor_of, own = 1.0, jax.random.fold_in(key, 6)
    for dim, shards_of in split:
        heights = jnp.exp(jax.random.uniform(jax.random.fold_in(own, dim), (shards_of,), jnp.float32, least / len(split), high / len(split)))
        factor_of = factor_of * jnp.repeat(heights, shape[dim] // shards_of).reshape([-1 if axis == dim else 1 for axis in range(len(shape))])
    return factor_of


def gaussian(key, dims, spread, bound, cuts=(), held_as=jnp.bfloat16):
    entries = spread * jax.random.normal(key, dims, jnp.float32)
    if cuts:
        entries = entries * levels(key, dims, cuts, -0.22, 0.18)
    return jnp.clip(entries, -bound, bound).astype(held_as)


def setup_inputs(seed: int = 0) -> dict:
    streams_of = jax.random.split(jax.random.key(seed), 8)
    voltages = gaussian(streams_of[0], (STATIONS, SPECTRA, 2 * POINTS), 1.0, 6.0, ((0, 128), (1, 4)))
    fir_taps = gaussian(streams_of[1], (TAPS, POINTS), 0.5, 3.0, (), jnp.float32)
    station_of_slot = jax.random.permutation(streams_of[2], STATIONS).astype(jnp.int32)
    station_u = with_ends(jax.random.randint(streams_of[3], (STATIONS,), 0, GRID), jax.random.fold_in(streams_of[3], 1), 0, GRID - 1).astype(jnp.int32)
    station_v = with_ends(jax.random.randint(streams_of[4], (STATIONS,), 0, GRID), jax.random.fold_in(streams_of[4], 1), 0, GRID - 1).astype(jnp.int32)
    pixel_l = with_ends(jax.random.randint(streams_of[5], (PIX_L,), 0 - GRID // 2, GRID // 2), jax.random.fold_in(streams_of[5], 1), 0 - GRID // 2, (GRID // 2) - 1).astype(jnp.int32)
    pixel_m = with_ends(jax.random.randint(streams_of[6], (PIX_M,), 0 - GRID // 2, GRID // 2), jax.random.fold_in(streams_of[6], 1), 0 - GRID // 2, (GRID // 2) - 1).astype(jnp.int32)
    return {"voltages": voltages, "fir_taps": fir_taps, "station_of_slot": station_of_slot, "station_u": station_u, "station_v": station_v, "pixel_l": pixel_l, "pixel_m": pixel_m}


def dft_matrix(points):
    counter = jnp.arange(points, dtype=jnp.int32)
    product = jnp.mod(counter[:, None] * counter[None, :], points).astype(jnp.float32)
    phase_angle = product * (2.0 * math.pi / points)
    cosine = jnp.cos(phase_angle)
    sine_part = jnp.sin(phase_angle)
    upper_rows = jnp.concatenate([cosine, sine_part], axis=1)
    lower_rows = jnp.concatenate([-sine_part, cosine], axis=1)
    return (jnp.concatenate([upper_rows, lower_rows], axis=0) * points ** (-0.5)).astype(jnp.bfloat16)

def steering(channel, station_u, station_v, rows_l, pixel_m):
    grid_phase = station_u[:, None, None] * rows_l[None, :, None] + station_v[:, None, None] * pixel_m[None, None, :]
    grid_phase = jnp.mod(grid_phase, GRID).reshape(station_u.shape[0], -1)
    phase_index = jnp.mod((POINTS + channel) * grid_phase, GRID)
    phase_angle = phase_index.astype(jnp.float32) * (2.0 * math.pi / GRID)
    return (jnp.cos(phase_angle).astype(jnp.bfloat16), jnp.sin(phase_angle).astype(jnp.bfloat16))

def reference(voltages, fir_taps, station_of_slot, station_u, station_v, pixel_l, pixel_m):
    taps_full = jnp.concatenate([fir_taps, fir_taps], axis=1).astype(jnp.float32)
    dft_table = dft_matrix(POINTS)

    def channelize(samples):
        padded = jnp.pad(samples.astype(jnp.float32), ((TAPS - 1, 0), (0, 0)))
        filtered = taps_full[0] * padded[TAPS - 1:TAPS - 1 + SPECTRA]
        for tap_index in range(1, TAPS):
            filtered = filtered + taps_full[tap_index] * padded[TAPS - 1 - tap_index:TAPS - 1 - tap_index + SPECTRA]
        filtered = filtered.astype(jnp.bfloat16)
        return jnp.dot(dft_table, filtered.T, preferred_element_type=jnp.float32).astype(jnp.bfloat16)
    spectra = lax.map(channelize, voltages)
    slot_of_station = jnp.zeros((STATIONS,), jnp.int32).at[station_of_slot].set(jnp.arange(STATIONS, dtype=jnp.int32))
    ordered = jnp.take(spectra, slot_of_station, axis=0).reshape(STATIONS, 2, POINTS, SPECTRA)
    inv_total = 1.0 / SPECTRA
    image_scale = math.sqrt(SPECTRA) / STATIONS
    diagonal = jnp.eye(STATIONS, dtype=bool)

    def one_channel(channel):
        real_part = lax.dynamic_index_in_dim(ordered[:, 0], channel, 1, keepdims=False)
        imag_part = lax.dynamic_index_in_dim(ordered[:, 1], channel, 1, keepdims=False)
        gram_real = jnp.dot(real_part, real_part.T, preferred_element_type=jnp.float32) + jnp.dot(imag_part, imag_part.T, preferred_element_type=jnp.float32)
        cross_gram = jnp.dot(imag_part, real_part.T, preferred_element_type=jnp.float32)
        vis_real = gram_real * inv_total
        vis_imag = (cross_gram - cross_gram.T) * inv_total
        flag_real = jnp.where(diagonal, 0.0, vis_real).astype(jnp.bfloat16)
        flag_imag = jnp.where(diagonal, 0.0, vis_imag).astype(jnp.bfloat16)
        cosine, sine_part = steering(channel, station_u, station_v, pixel_l, pixel_m)
        weight_real = jnp.dot(flag_real, cosine, preferred_element_type=jnp.float32) + jnp.dot(flag_imag, sine_part, preferred_element_type=jnp.float32)
        weight_imag = jnp.dot(flag_imag, cosine, preferred_element_type=jnp.float32) - jnp.dot(flag_real, sine_part, preferred_element_type=jnp.float32)
        pixels_out = lax.optimization_barrier(jnp.sum(cosine.astype(jnp.float32) * weight_real - sine_part.astype(jnp.float32) * weight_imag, axis=0)) * image_scale
        return (jnp.stack([vis_real, vis_imag]), pixels_out)
    visibilities, image = lax.map(one_channel, jnp.arange(POINTS, dtype=jnp.int32))
    return (visibilities, image)
```

```python
import math

import jax
import jax.numpy as jnp
import numpy as np
from jax import lax
from jax.experimental import pallas as pl
from jax.experimental.pallas import tpu as pltpu
from jax.sharding import PartitionSpec as P

POINTS = 128
TAPS = 4
GRID = 1024
LANES = 128
STATIONS = 256
HALO = 8

VMEM = pl.BlockSpec(memory_space=pltpu.VMEM)
SMEM = pl.BlockSpec(memory_space=pltpu.SMEM)
F32 = jnp.float32
BF16 = jnp.bfloat16


def dft_matrix(points):
    counter = np.arange(points)
    angle = np.mod(counter[:, None] * counter[None, :], points) * (2.0 * math.pi / points)
    cosine, sine = np.cos(angle), np.sin(angle)
    table = np.block([[cosine, sine], [-sine, cosine]]) * points ** (-0.5)
    return jnp.asarray(table, dtype=F32).astype(BF16)


def params(flops, moved):
    return dict(
        compiler_params=pltpu.CompilerParams(vmem_limit_bytes=40 * 1024 * 1024),
        cost_estimate=pl.CostEstimate(flops=flops, bytes_accessed=moved, transcendentals=0),
    )


def filter_kernel(v_ref, hist_ref, taps_ref, dft_ref, out_ref, ext, wide):
    spec_dev = v_ref.shape[1]
    taps = jnp.concatenate([taps_ref[...], taps_ref[...]], axis=1)
    step = 256
    for s in range(2):
        ext[s, 0:HALO, :] = hist_ref[s].astype(F32)
        ext[s, HALO:, :] = v_ref[s].astype(F32)
    for s in range(2):
        for t in range(0, spec_dev, step):
            total = taps[0:1] * ext[s, HALO + t : HALO + t + step, :]
            for k in range(1, TAPS):
                total = total + taps[k : k + 1] * ext[s, HALO - k + t : HALO - k + t + step, :]
            spectra = lax.dot_general(
                dft_ref[...], total.astype(BF16), (((1,), (1,)), ((), ())), preferred_element_type=F32
            )
            for r in range(2):
                for part in range(step // LANES):
                    row = s * 8 + r * 4 + t // LANES + part
                    wide[pl.ds(row, POINTS, stride=16), :] = spectra[
                        r * POINTS : (r + 1) * POINTS, part * LANES : (part + 1) * LANES
                    ]
    for c in range(0, POINTS, 16):
        out_ref[c : c + 16] = wide[c * 16 : (c + 16) * 16, :].astype(BF16).reshape(16, 16, LANES)


def filter_bank(voltages, history, fir_taps):
    return pl.pallas_call(
        filter_kernel,
        out_shape=jax.ShapeDtypeStruct((POINTS, 16, LANES), BF16),
        in_specs=[VMEM] * 4,
        out_specs=VMEM,
        scratch_shapes=[
            pltpu.VMEM((2, HALO + voltages.shape[1], 2 * POINTS), F32),
            pltpu.VMEM((POINTS * 16, LANES), F32),
        ],
        name="filter_bank",
        **params(2 * 256 * 256 * 1024, 1 << 20),
    )(voltages, history, fir_taps, dft_matrix(POINTS))


def steering_kernel(chan_ref, u_ref, v_ref, l_ref, m_ref, cos_ref, sin_ref):
    freq = POINTS + chan_ref[0]
    rows = lax.broadcasted_iota(jnp.int32, (STATIONS, STATIONS), 0)
    cols = lax.broadcasted_iota(jnp.int32, (STATIONS, STATIONS), 1)
    eye = rows == cols

    def column(ref):
        return jnp.sum(jnp.where(eye, ref[...], 0), axis=1, keepdims=True)

    def phases(station, pixel):
        index = (freq * ((station * pixel) & (GRID - 1))) & (GRID - 1)
        angle = index.astype(F32) * (2.0 * math.pi / GRID)
        return jnp.cos(angle), jnp.sin(angle)

    l_cos, l_sin = phases(column(u_ref), l_ref[...])
    m_cos, m_sin = phases(column(v_ref), m_ref[...])
    first = lax.broadcasted_iota(jnp.int32, (STATIONS, LANES), 1) < 64
    for q in range(cos_ref.shape[1] // LANES):
        a_cos = jnp.where(first, l_cos[:, 2 * q : 2 * q + 1], l_cos[:, 2 * q + 1 : 2 * q + 2])
        a_sin = jnp.where(first, l_sin[:, 2 * q : 2 * q + 1], l_sin[:, 2 * q + 1 : 2 * q + 2])
        cos_ref[:, q * LANES : (q + 1) * LANES] = (a_cos * m_cos - a_sin * m_sin).astype(BF16)
        sin_ref[:, q * LANES : (q + 1) * LANES] = (a_sin * m_cos + a_cos * m_sin).astype(BF16)


def steering(channel, station_u, station_v, rows_l, pixel_m, pixels):
    out = jax.ShapeDtypeStruct((STATIONS, pixels), BF16)
    return pl.pallas_call(
        steering_kernel,
        out_shape=(out, out),
        in_specs=[SMEM] + [VMEM] * 4,
        out_specs=(VMEM, VMEM),
        name="steering",
        **params(6 * STATIONS * pixels, 4 * STATIONS * pixels),
    )(channel, station_u, station_v, rows_l, pixel_m)


def gram_kernel(recv_ref, station_ref, out_ref, wide, slots):
    for c in range(0, POINTS, 16):
        wide[c * 16 : (c + 16) * 16, :] = recv_ref[c : c + 16].reshape(256, LANES).astype(F32)
    for s in range(2):
        for q in range(8):
            slots[s * POINTS : (s + 1) * POINTS, q * LANES : (q + 1) * LANES] = wide[
                pl.ds(s * 8 + q, POINTS, stride=16), :
            ].astype(BF16)
    rows = lax.broadcasted_iota(jnp.int32, (STATIONS, STATIONS), 0)
    select = jnp.where(rows == station_ref[...], 1.0, 0.0).astype(BF16)
    ordered = jnp.dot(select, slots[...], preferred_element_type=F32).astype(BF16)
    half = ordered.shape[1] // 2
    turned = jnp.concatenate([ordered[:, half:], -ordered[:, :half]], axis=1)
    contract = (((1,), (1,)), ((), ()))
    out_ref[0] = lax.dot_general(ordered, ordered, contract, preferred_element_type=F32).astype(BF16)
    out_ref[1] = lax.dot_general(turned, ordered, contract, preferred_element_type=F32).astype(BF16)


def gram(received, station_row):
    return pl.pallas_call(
        gram_kernel,
        out_shape=jax.ShapeDtypeStruct((2, STATIONS, STATIONS), BF16),
        in_specs=[VMEM] * 2,
        out_specs=VMEM,
        scratch_shapes=[
            pltpu.VMEM((POINTS * 16, LANES), F32),
            pltpu.VMEM((STATIONS, 1024), BF16),
        ],
        name="gram",
        **params(6 * 256 * 256 * 1024, 1 << 20),
    )(received, station_row)


def image_kernel(place_ref, own_ref, other_ref, cos_ref, sin_ref, rows_ref, pixels_ref, send_ref, real, imag):
    rows = lax.broadcasted_iota(jnp.int32, (STATIONS, STATIONS), 0)
    cols = lax.broadcasted_iota(jnp.int32, (STATIONS, STATIONS), 1)
    real[...] = own_ref[0].astype(F32) + other_ref[0].astype(F32)
    imag[...] = own_ref[1].astype(F32) + other_ref[1].astype(F32)
    count = rows_ref.shape[1]
    here = pl.ds(pl.multiple_of(place_ref[0] * count, count), count)
    across = pl.ds(pl.multiple_of(place_ref[1] * count, count), count)
    rows_ref[0] = real[here, :]
    rows_ref[1] = imag[here, :]
    send_ref[0:count, :] = real[across, :].astype(BF16)
    send_ref[count : 2 * count, :] = imag[across, :].astype(BF16)
    flag_real = jnp.where(rows == cols, 0.0, real[...]).astype(BF16)
    flag_imag = jnp.where(rows == cols, 0.0, imag[...]).astype(BF16)
    width = 256
    groups = cos_ref.shape[1] // width
    for q in range(groups):
        cosine = cos_ref[:, q * width : (q + 1) * width]
        sine = sin_ref[:, q * width : (q + 1) * width]
        upper = jnp.dot(flag_real, cosine, preferred_element_type=F32) + 2.0 * jnp.dot(
            flag_imag, sine, preferred_element_type=F32
        )
        lower = jnp.dot(flag_real, sine, preferred_element_type=F32)
        pixel = jnp.sum(cosine.astype(F32) * upper + sine.astype(F32) * lower, axis=0, keepdims=True)
        if q < groups // 2:
            pixels_ref[q : q + 1, :] = pixel
        else:
            at = 2 * count + q - groups // 2
            send_ref[at : at + 1, :] = pixel.astype(BF16)
    send_ref[2 * count + groups // 2 :, :] = jnp.zeros_like(send_ref[2 * count + groups // 2 :, :])


def image_rows(place, own, other, cosine, sine, count):
    groups = cosine.shape[1] // 512
    return pl.pallas_call(
        image_kernel,
        out_shape=(
            jax.ShapeDtypeStruct((2, count, STATIONS), F32),
            jax.ShapeDtypeStruct((groups, STATIONS), F32),
            jax.ShapeDtypeStruct((2 * count + 16, STATIONS), BF16),
        ),
        in_specs=[SMEM] + [VMEM] * 4,
        out_specs=(VMEM, VMEM, VMEM),
        scratch_shapes=[pltpu.VMEM((STATIONS, STATIONS), F32)] * 2,
        name="image_rows",
        **params(6 * 256 * 256 * 2048, 1 << 21),
    )(place, own, other, cosine, sine)


def finish_kernel(inv_total, image_scale, rows_ref, pixels_ref, got_ref, vis_ref, image_ref):
    count = rows_ref.shape[1]
    for part in range(2):
        got = got_ref[part * count : (part + 1) * count, :].astype(F32)
        vis_ref[0, part] = (rows_ref[part] + got) * inv_total
    for q in range(pixels_ref.shape[0]):
        got = got_ref[2 * count + q : 2 * count + q + 1, :].astype(F32)
        image_ref[:, q * STATIONS : (q + 1) * STATIONS] = (pixels_ref[q : q + 1, :] + got) * (
            inv_total * image_scale
        )


def finish(rows, pixels, got, inv_total, image_scale):
    count = rows.shape[1]
    return pl.pallas_call(
        lambda *refs: finish_kernel(inv_total, image_scale, *refs),
        out_shape=(
            jax.ShapeDtypeStruct((1, 2, count, STATIONS), F32),
            jax.ShapeDtypeStruct((1, pixels.size), F32),
        ),
        in_specs=[VMEM] * 3,
        out_specs=(VMEM, VMEM),
        name="finish",
        **params(1 << 16, 1 << 18),
    )(rows, pixels, got)


def on_device(voltages, fir_taps, station_of_slot, station_u, station_v, pixel_l, pixel_m):
    spec_dev = voltages.shape[1]
    pix_count = lax.axis_size("pix")
    spectra_total = spec_dev * pix_count
    pix = lax.axis_index("pix")
    across = jnp.where(pix < 2, pix + 2, pix - 2)
    rows_l = pixel_l.shape[0] // pix_count
    history = lax.ppermute(
        voltages[:, spec_dev - HALO :, :], "pix", [(i, i + 1) for i in range(pix_count - 1)]
    )
    sent = filter_bank(voltages, history, fir_taps)
    received = lax.all_to_all(sent, "chan", split_axis=0, concat_axis=0, tiled=True)

    block_l = jnp.concatenate(
        [
            lax.dynamic_slice_in_dim(pixel_l, pix * rows_l, rows_l, 0),
            lax.dynamic_slice_in_dim(pixel_l, across * rows_l, rows_l, 0),
            jnp.zeros((LANES - 2 * rows_l,), jnp.int32),
        ]
    )[None]
    cosine, sine = steering(
        lax.axis_index("chan")[None].astype(jnp.int32),
        station_u[None],
        station_v[None],
        block_l,
        jnp.concatenate([pixel_m, pixel_m])[None],
        2 * rows_l * pixel_m.shape[0],
    )
    station_row = station_of_slot.reshape(POINTS, 2).T.reshape(1, STATIONS)
    own = gram(received, station_row)
    other = lax.ppermute(own, "pix", [(0, 1), (1, 0), (2, 3), (3, 2)])
    place = jnp.stack([pix, across]).astype(jnp.int32)
    rows, pixels, send = image_rows(place, own, other, cosine, sine, STATIONS // pix_count)
    got = lax.ppermute(send, "pix", [(0, 2), (2, 0), (1, 3), (3, 1)])
    return finish(rows, pixels, got, 1.0 / spectra_total, math.sqrt(spectra_total) / STATIONS)


def solution(mesh):
    in_specs = (P("chan", "pix", None), P(), P(), P(), P(), P(), P())
    out_specs = (P("chan", None, "pix", None), P("chan", "pix"))
    return jax.shard_map(
        on_device, mesh=mesh, in_specs=in_specs, out_specs=out_specs, check_vma=False
    )
```

```python
import math

import jax
import jax.numpy as jnp
import numpy as np
from jax import lax
from jax.experimental import pallas as pl
from jax.experimental.pallas import tpu as pltpu
from jax.sharding import PartitionSpec as P

POINTS = 128
TAPS = 4
GRID = 1024
LANES = 128
STATIONS = 256
HALO = 8

VMEM = pl.BlockSpec(memory_space=pltpu.VMEM)
HBM = pl.BlockSpec(memory_space=pltpu.HBM)
ANY = pl.BlockSpec(memory_space=pl.ANY)
SMEM = pl.BlockSpec(memory_space=pltpu.SMEM)
F32 = jnp.float32
BF16 = jnp.bfloat16


def dft_matrix(points):
    counter = np.arange(points)
    angle = np.mod(counter[:, None] * counter[None, :], points) * (2.0 * math.pi / points)
    cosine, sine = np.cos(angle), np.sin(angle)
    table = np.block([[cosine, sine], [-sine, cosine]]) * points ** (-0.5)
    return jnp.asarray(table, dtype=F32).astype(BF16)


def params(flops, moved):
    return dict(
        compiler_params=pltpu.CompilerParams(vmem_limit_bytes=40 * 1024 * 1024),
        cost_estimate=pl.CostEstimate(flops=flops, bytes_accessed=moved, transcendentals=0),
    )


def filter_kernel(v_hbm, hist_ref, taps_ref, dft_hbm, out_ref, v_ref, dft_ref, ext, wide, sems):
    spec_dev = v_ref.shape[1]
    copies = [pltpu.make_async_copy(v_hbm.at[s], v_ref.at[s], sems.at[s]) for s in range(2)]
    copies.append(pltpu.make_async_copy(dft_hbm, dft_ref, sems.at[2]))
    for copy in copies:
        copy.start()
    taps = jnp.concatenate([taps_ref[...], taps_ref[...]], axis=1)
    step = 256
    for s in range(2):
        ext[s, 0:HALO, :] = hist_ref[s].astype(F32)
        copies[s].wait()
        ext[s, HALO:, :] = v_ref[s].astype(F32)
        if s == 0:
            copies[2].wait()
        for t in range(0, spec_dev, step):
            total = taps[0:1] * ext[s, HALO + t : HALO + t + step, :]
            for k in range(1, TAPS):
                total = total + taps[k : k + 1] * ext[s, HALO - k + t : HALO - k + t + step, :]
            spectra = lax.dot_general(
                dft_ref[...], total.astype(BF16), (((1,), (1,)), ((), ())), preferred_element_type=F32
            )
            for r in range(2):
                for part in range(step // LANES):
                    row = s * 8 + r * 4 + t // LANES + part
                    wide[pl.ds(row, POINTS, stride=16), :] = spectra[
                        r * POINTS : (r + 1) * POINTS, part * LANES : (part + 1) * LANES
                    ]
    for c in range(0, POINTS, 16):
        out_ref[c : c + 16] = wide[c * 16 : (c + 16) * 16, :].astype(BF16).reshape(16, 16, LANES)


def filter_bank(voltages, history, fir_taps):
    return pl.pallas_call(
        filter_kernel,
        out_shape=jax.ShapeDtypeStruct((POINTS, 16, LANES), BF16),
        in_specs=[HBM, VMEM, VMEM, HBM],
        out_specs=VMEM,
        scratch_shapes=[
            pltpu.VMEM(voltages.shape, BF16),
            pltpu.VMEM((2 * POINTS, 2 * POINTS), BF16),
            pltpu.VMEM((2, HALO + voltages.shape[1], 2 * POINTS), F32),
            pltpu.VMEM((POINTS * 16, LANES), F32),
            pltpu.SemaphoreType.DMA((3,)),
        ],
        name="filter_bank",
        **params(2 * 256 * 256 * 1024, 1 << 20),
    )(voltages, history, fir_taps, dft_matrix(POINTS))


def steering_kernel(chan_ref, u_ref, v_ref, l_ref, m_ref, cos_ref, sin_ref):
    freq = POINTS + chan_ref[0]
    rows = lax.broadcasted_iota(jnp.int32, (STATIONS, STATIONS), 0)
    cols = lax.broadcasted_iota(jnp.int32, (STATIONS, STATIONS), 1)
    eye = rows == cols

    def column(ref):
        return jnp.sum(jnp.where(eye, ref[...], 0), axis=1, keepdims=True)

    def phases(station, pixel):
        index = (freq * ((station * pixel) & (GRID - 1))) & (GRID - 1)
        angle = index.astype(F32) * (2.0 * math.pi / GRID)
        return jnp.cos(angle), jnp.sin(angle)

    l_cos, l_sin = phases(column(u_ref), l_ref[...])
    m_cos, m_sin = phases(column(v_ref), m_ref[...])
    first = lax.broadcasted_iota(jnp.int32, (STATIONS, LANES), 1) < 64
    for q in range(cos_ref.shape[1] // LANES):
        a_cos = jnp.where(first, l_cos[:, 2 * q : 2 * q + 1], l_cos[:, 2 * q + 1 : 2 * q + 2])
        a_sin = jnp.where(first, l_sin[:, 2 * q : 2 * q + 1], l_sin[:, 2 * q + 1 : 2 * q + 2])
        cos_ref[:, q * LANES : (q + 1) * LANES] = (a_cos * m_cos - a_sin * m_sin).astype(BF16)
        sin_ref[:, q * LANES : (q + 1) * LANES] = (a_sin * m_cos + a_cos * m_sin).astype(BF16)


def steering(channel, station_u, station_v, rows_l, pixel_m, pixels):
    out = jax.ShapeDtypeStruct((STATIONS, pixels), BF16)
    return pl.pallas_call(
        steering_kernel,
        out_shape=(out, out),
        in_specs=[SMEM] + [VMEM] * 4,
        out_specs=(VMEM, VMEM),
        name="steering",
        **params(6 * STATIONS * pixels, 4 * STATIONS * pixels),
    )(channel, station_u, station_v, rows_l, pixel_m)


def gram_kernel(recv_ref, station_ref, after_ref, out_ref, wide, slots):
    for c in range(0, POINTS, 16):
        wide[c * 16 : (c + 16) * 16, :] = recv_ref[c : c + 16].reshape(256, LANES).astype(F32)
    for s in range(2):
        for q in range(8):
            slots[s * POINTS : (s + 1) * POINTS, q * LANES : (q + 1) * LANES] = wide[
                pl.ds(s * 8 + q, POINTS, stride=16), :
            ].astype(BF16)
    rows = lax.broadcasted_iota(jnp.int32, (STATIONS, STATIONS), 0)
    select = jnp.where(rows == station_ref[...], 1.0, 0.0).astype(BF16)
    ordered = jnp.dot(select, slots[...], preferred_element_type=F32).astype(BF16)
    half = ordered.shape[1] // 2
    turned = jnp.concatenate([ordered[:, half:], -ordered[:, :half]], axis=1)
    contract = (((1,), (1,)), ((), ()))
    out_ref[0] = lax.dot_general(ordered, ordered, contract, preferred_element_type=F32).astype(BF16)
    out_ref[1] = lax.dot_general(turned, ordered, contract, preferred_element_type=F32).astype(BF16)


def gram(received, station_row, after):
    return pl.pallas_call(
        gram_kernel,
        out_shape=jax.ShapeDtypeStruct((2, STATIONS, STATIONS), BF16),
        in_specs=[VMEM, VMEM, ANY],
        out_specs=VMEM,
        scratch_shapes=[
            pltpu.VMEM((POINTS * 16, LANES), F32),
            pltpu.VMEM((STATIONS, 1024), BF16),
        ],
        name="gram",
        **params(6 * 256 * 256 * 1024, 1 << 20),
    )(received, station_row, after)


def image_kernel(place_ref, own_ref, other_ref, cos_ref, sin_ref, rows_ref, pixels_ref, send_ref, real, imag):
    rows = lax.broadcasted_iota(jnp.int32, (STATIONS, STATIONS), 0)
    cols = lax.broadcasted_iota(jnp.int32, (STATIONS, STATIONS), 1)
    real[...] = own_ref[0].astype(F32) + other_ref[0].astype(F32)
    imag[...] = own_ref[1].astype(F32) + other_ref[1].astype(F32)
    count = rows_ref.shape[1]
    here = pl.ds(pl.multiple_of(place_ref[0] * count, count), count)
    across = pl.ds(pl.multiple_of(place_ref[1] * count, count), count)
    rows_ref[0] = real[here, :]
    rows_ref[1] = imag[here, :]
    send_ref[0:count, :] = real[across, :].astype(BF16)
    send_ref[count : 2 * count, :] = imag[across, :].astype(BF16)
    flag_real = jnp.where(rows == cols, 0.0, real[...]).astype(BF16)
    flag_imag = jnp.where(rows == cols, 0.0, imag[...]).astype(BF16)
    width = 256
    groups = cos_ref.shape[1] // width
    for q in range(groups):
        cosine = cos_ref[:, q * width : (q + 1) * width]
        sine = sin_ref[:, q * width : (q + 1) * width]
        upper = jnp.dot(flag_real, cosine, preferred_element_type=F32) + 2.0 * jnp.dot(
            flag_imag, sine, preferred_element_type=F32
        )
        lower = jnp.dot(flag_real, sine, preferred_element_type=F32)
        pixel = jnp.sum(cosine.astype(F32) * upper + sine.astype(F32) * lower, axis=0, keepdims=True)
        if q < groups // 2:
            pixels_ref[q : q + 1, :] = pixel
        else:
            at = 2 * count + q - groups // 2
            send_ref[at : at + 1, :] = pixel.astype(BF16)
    send_ref[2 * count + groups // 2 :, :] = jnp.zeros_like(send_ref[2 * count + groups // 2 :, :])


def image_rows(place, own, other, cosine, sine, count):
    groups = cosine.shape[1] // 512
    return pl.pallas_call(
        image_kernel,
        out_shape=(
            jax.ShapeDtypeStruct((2, count, STATIONS), F32),
            jax.ShapeDtypeStruct((groups, STATIONS), F32),
            jax.ShapeDtypeStruct((2 * count + 16, STATIONS), BF16),
        ),
        in_specs=[SMEM] + [VMEM] * 4,
        out_specs=(VMEM, VMEM, VMEM),
        scratch_shapes=[pltpu.VMEM((STATIONS, STATIONS), F32)] * 2,
        name="image_rows",
        **params(6 * 256 * 256 * 2048, 1 << 21),
    )(place, own, other, cosine, sine)


def finish_kernel(inv_total, image_scale, rows_ref, pixels_ref, got_ref, vis_ref, image_ref):
    count = rows_ref.shape[1]
    for part in range(2):
        got = got_ref[part * count : (part + 1) * count, :].astype(F32)
        vis_ref[0, part] = (rows_ref[part] + got) * inv_total
    for q in range(pixels_ref.shape[0]):
        got = got_ref[2 * count + q : 2 * count + q + 1, :].astype(F32)
        image_ref[:, q * STATIONS : (q + 1) * STATIONS] = (pixels_ref[q : q + 1, :] + got) * (
            inv_total * image_scale
        )


def finish(rows, pixels, got, inv_total, image_scale):
    count = rows.shape[1]
    return pl.pallas_call(
        lambda *refs: finish_kernel(inv_total, image_scale, *refs),
        out_shape=(
            jax.ShapeDtypeStruct((1, 2, count, STATIONS), F32),
            jax.ShapeDtypeStruct((1, pixels.size), F32),
        ),
        in_specs=[VMEM] * 3,
        out_specs=(VMEM, VMEM),
        name="finish",
        **params(1 << 16, 1 << 18),
    )(rows, pixels, got)


def on_device(voltages, fir_taps, station_of_slot, station_u, station_v, pixel_l, pixel_m):
    spec_dev = voltages.shape[1]
    pix_count = lax.axis_size("pix")
    spectra_total = spec_dev * pix_count
    pix = lax.axis_index("pix")
    across = jnp.where(pix < 2, pix + 2, pix - 2)
    rows_l = pixel_l.shape[0] // pix_count
    history = lax.ppermute(
        voltages[:, spec_dev - HALO :, :], "pix", [(i, i + 1) for i in range(pix_count - 1)]
    )
    sent = filter_bank(voltages, history, fir_taps)
    received = lax.all_to_all(sent, "chan", split_axis=0, concat_axis=0, tiled=True)

    block_l = jnp.concatenate(
        [
            lax.dynamic_slice_in_dim(pixel_l, pix * rows_l, rows_l, 0),
            lax.dynamic_slice_in_dim(pixel_l, across * rows_l, rows_l, 0),
            jnp.zeros((LANES - 2 * rows_l,), jnp.int32),
        ]
    )[None]
    cosine, sine = steering(
        lax.axis_index("chan")[None].astype(jnp.int32),
        station_u[None],
        station_v[None],
        block_l,
        jnp.concatenate([pixel_m, pixel_m])[None],
        2 * rows_l * pixel_m.shape[0],
    )
    station_row = station_of_slot.reshape(POINTS, 2).T.reshape(1, STATIONS)
    own = gram(received, station_row, cosine)
    other = lax.ppermute(own, "pix", [(0, 1), (1, 0), (2, 3), (3, 2)])
    place = jnp.stack([pix, across]).astype(jnp.int32)
    rows, pixels, send = image_rows(place, own, other, cosine, sine, STATIONS // pix_count)
    got = lax.ppermute(send, "pix", [(0, 2), (2, 0), (1, 3), (3, 1)])
    return finish(rows, pixels, got, 1.0 / spectra_total, math.sqrt(spectra_total) / STATIONS)


def solution(mesh):
    in_specs = (P("chan", "pix", None), P(), P(), P(), P(), P(), P())
    out_specs = (P("chan", None, "pix", None), P("chan", "pix"))
    return jax.shard_map(
        on_device, mesh=mesh, in_specs=in_specs, out_specs=out_specs, check_vma=False
    )
```

```python
import math

import jax
import jax.numpy as jnp
import numpy as np
from jax import lax
from jax.experimental import pallas as pl
from jax.experimental.pallas import tpu as pltpu
from jax.sharding import PartitionSpec as P

POINTS = 128
TAPS = 4
GRID = 1024
LANES = 128
STATIONS = 256
EDGE = 8
ROWS = 18

VMEM = pl.BlockSpec(memory_space=pltpu.VMEM)
HBM = pl.BlockSpec(memory_space=pltpu.HBM)
ANY = pl.BlockSpec(memory_space=pl.ANY)
SMEM = pl.BlockSpec(memory_space=pltpu.SMEM)
F32 = jnp.float32
BF16 = jnp.bfloat16


def dft_matrix(points):
    counter = np.arange(points)
    angle = np.mod(counter[:, None] * counter[None, :], points) * (2.0 * math.pi / points)
    cosine, sine = np.cos(angle), np.sin(angle)
    table = np.block([[cosine, sine], [-sine, cosine]]) * points ** (-0.5)
    return jnp.asarray(table, dtype=F32).astype(BF16)


def params(flops, moved, limit=40 * 1024 * 1024):
    return dict(
        compiler_params=pltpu.CompilerParams(vmem_limit_bytes=limit),
        cost_estimate=pl.CostEstimate(flops=flops, bytes_accessed=moved, transcendentals=0),
    )


def filter_kernel(v_hbm, taps_ref, dft_hbm, out_hbm, v_ref, dft_ref, ext, tail, wide, packed, sems):
    spec_dev = v_hbm.shape[1]
    copies = [pltpu.make_async_copy(v_hbm.at[s], v_ref.at[s], sems.at[s]) for s in range(2)]
    copies.append(pltpu.make_async_copy(dft_hbm, dft_ref, sems.at[2]))
    for copy in copies:
        copy.start()
    taps = jnp.concatenate([taps_ref[...], taps_ref[...]], axis=1)
    step = 256
    contract = (((1,), (1,)), ((), ()))
    for s in range(2):
        ext[s, 0:EDGE, :] = jnp.zeros((EDGE, 2 * POINTS), F32)
        ext[s, EDGE + spec_dev :, :] = jnp.zeros((EDGE, 2 * POINTS), F32)
    tail[2 * EDGE :, :] = jnp.zeros((LANES - 2 * EDGE, 2 * POINTS), BF16)

    def filtered(s, start, count):
        total = taps[0:1] * ext[s, EDGE + start : EDGE + start + count, :]
        for k in range(1, TAPS):
            total = total + taps[k : k + 1] * ext[s, EDGE - k + start : EDGE - k + start + count, :]
        return total

    for s in range(2):
        copies[s].wait()
        ext[s, EDGE : EDGE + spec_dev, :] = v_ref[s].astype(F32)
        if s == 0:
            copies[2].wait()
        for t in range(0, spec_dev, step):
            spectra = lax.dot_general(
                dft_ref[...], filtered(s, t, step).astype(BF16), contract, preferred_element_type=F32
            )
            for r in range(2):
                for part in range(step // LANES):
                    row = s * 8 + r * 4 + t // LANES + part
                    wide[pl.ds(row, POINTS, stride=ROWS), :] = spectra[
                        r * POINTS : (r + 1) * POINTS, part * LANES : (part + 1) * LANES
                    ]
    edges = jnp.concatenate([filtered(s, spec_dev, EDGE) for s in range(2)], axis=0)
    tail[0 : 2 * EDGE, :] = edges.astype(BF16)
    spectra = lax.dot_general(dft_ref[...], tail[...], contract, preferred_element_type=F32)
    for r in range(2):
        wide[pl.ds(16 + r, POINTS, stride=ROWS), :] = spectra[r * POINTS : (r + 1) * POINTS]
    chunk = POINTS * ROWS // 8
    writes = []
    for c in range(8):
        here = pl.ds(c * chunk // 2, chunk // 2)
        packed[here] = wide[c * chunk : (c + 1) * chunk, :].astype(BF16).reshape(chunk // 2, 2, LANES)
        writes.append(pltpu.make_async_copy(packed.at[here], out_hbm.at[here], sems.at[3 + c]))
        writes[-1].start()
    for write in writes:
        write.wait()


def filter_bank(voltages, fir_taps):
    pairs = POINTS * ROWS // 2
    return pl.pallas_call(
        filter_kernel,
        out_shape=jax.ShapeDtypeStruct((pairs, 2, LANES), BF16),
        in_specs=[HBM, VMEM, HBM],
        out_specs=HBM,
        scratch_shapes=[
            pltpu.VMEM(voltages.shape, BF16),
            pltpu.VMEM((2 * POINTS, 2 * POINTS), BF16),
            pltpu.VMEM((2, 2 * EDGE + voltages.shape[1], 2 * POINTS), F32),
            pltpu.VMEM((LANES, 2 * POINTS), BF16),
            pltpu.VMEM((2 * pairs, LANES), F32),
            pltpu.VMEM((pairs, 2, LANES), BF16),
            pltpu.SemaphoreType.DMA((11,)),
        ],
        name="filter_bank",
        **params(2 * 256 * 256 * 1024, 1 << 20, 66_000_000),
    )(voltages, fir_taps, dft_matrix(POINTS))


def steering_kernel(chan_ref, u_ref, v_ref, l_ref, m_ref, cos_ref, sin_ref):
    freq = POINTS + chan_ref[0]
    rows = lax.broadcasted_iota(jnp.int32, (STATIONS, STATIONS), 0)
    cols = lax.broadcasted_iota(jnp.int32, (STATIONS, STATIONS), 1)
    eye = rows == cols

    def column(ref):
        return jnp.sum(jnp.where(eye, ref[...], 0), axis=1, keepdims=True)

    def phases(station, pixel):
        index = (freq * ((station * pixel) & (GRID - 1))) & (GRID - 1)
        angle = index.astype(F32) * (2.0 * math.pi / GRID)
        return jnp.cos(angle), jnp.sin(angle)

    l_cos, l_sin = phases(column(u_ref), l_ref[...])
    m_cos, m_sin = phases(column(v_ref), m_ref[...])
    first = lax.broadcasted_iota(jnp.int32, (STATIONS, LANES), 1) < 64
    for q in range(cos_ref.shape[1] // LANES):
        a_cos = jnp.where(first, l_cos[:, 2 * q : 2 * q + 1], l_cos[:, 2 * q + 1 : 2 * q + 2])
        a_sin = jnp.where(first, l_sin[:, 2 * q : 2 * q + 1], l_sin[:, 2 * q + 1 : 2 * q + 2])
        cos_ref[:, q * LANES : (q + 1) * LANES] = (a_cos * m_cos - a_sin * m_sin).astype(BF16)
        sin_ref[:, q * LANES : (q + 1) * LANES] = (a_sin * m_cos + a_cos * m_sin).astype(BF16)


def steering(channel, station_u, station_v, rows_l, pixel_m, pixels):
    out = jax.ShapeDtypeStruct((STATIONS, pixels), BF16)
    return pl.pallas_call(
        steering_kernel,
        out_shape=(out, out),
        in_specs=[SMEM] + [VMEM] * 4,
        out_specs=(VMEM, VMEM),
        name="steering",
        **params(6 * STATIONS * pixels, 4 * STATIONS * pixels),
    )(channel, station_u, station_v, rows_l, pixel_m)


def gram_kernel(place_ref, recv_ref, station_ref, after_ref, out_ref, wide, slots):
    chunk = 256
    for c in range(0, POINTS * ROWS, chunk):
        wide[c : c + chunk, :] = recv_ref[c // 2 : (c + chunk) // 2].reshape(chunk, LANES).astype(F32)
    lane = lax.broadcasted_iota(jnp.int32, (POINTS, LANES), 1)
    head = lane < TAPS - 1
    edge = lane < EDGE
    left_out = jnp.logical_and(head, place_ref[0] > 0)

    def column(row):
        return wide[pl.ds(row, POINTS, stride=ROWS), :]

    for s in range(2):
        rows = slice(s * POINTS, (s + 1) * POINTS)
        for q in range(8):
            values = column(s * 8 + q)
            if q % 4 == 0:
                values = jnp.where(left_out, 0.0, values)
            slots[rows, q * LANES : (q + 1) * LANES] = values.astype(BF16)
        pieces = [
            pltpu.roll(column(16 + r), LANES - EDGE, 1) if s else column(16 + r) for r in range(2)
        ]
        pieces = [jnp.where(edge, piece, 0.0) for piece in pieces]
        pieces += [jnp.where(head, column(s * 8 + r * 4), 0.0) for r in range(2)]
        total = pieces[0]
        for i in range(1, 4):
            total = total + pltpu.roll(pieces[i], i * EDGE, 1)
        slots[rows, 8 * LANES :] = total.astype(BF16)
    rows = lax.broadcasted_iota(jnp.int32, (STATIONS, STATIONS), 0)
    select = jnp.where(rows == station_ref[...], 1.0, 0.0).astype(BF16)
    ordered = jnp.dot(select, slots[...], preferred_element_type=F32).astype(BF16)
    half = 4 * LANES
    spectra = ordered[:, : 2 * half]
    turned = jnp.concatenate([ordered[:, half : 2 * half], -ordered[:, :half]], axis=1)
    contract = (((1,), (1,)), ((), ()))
    real = lax.dot_general(spectra, spectra, contract, preferred_element_type=F32)
    imag = lax.dot_general(turned, spectra, contract, preferred_element_type=F32)
    out_ref[:, 0:STATIONS] = real.astype(BF16)
    out_ref[:, STATIONS : 2 * STATIONS] = imag.astype(BF16)
    out_ref[:, 2 * STATIONS :] = ordered[:, 2 * half :]


def gram(place, received, station_row, after):
    return pl.pallas_call(
        gram_kernel,
        out_shape=jax.ShapeDtypeStruct((STATIONS, 2 * STATIONS + LANES), BF16),
        in_specs=[SMEM, VMEM, VMEM, ANY],
        out_specs=VMEM,
        scratch_shapes=[
            pltpu.VMEM((POINTS * ROWS, LANES), F32),
            pltpu.VMEM((STATIONS, 9 * LANES), BF16),
        ],
        name="gram",
        **params(6 * 256 * 256 * 1024, 1 << 20),
    )(place, received, station_row, after)


def image_kernel(place_ref, own_ref, other_ref, cos_ref, sin_ref, rows_ref, extra_ref, send_ref, real, imag):
    count = rows_ref.shape[1]
    lane = lax.broadcasted_iota(jnp.int32, (STATIONS, LANES), 1)
    contract = (((1,), (1,)), ((), ()))
    upper_core = (place_ref[0] & 1) == 1
    second_chip = place_ref[0] >= 2
    own_edge = own_ref[:, 2 * STATIONS :].astype(F32)
    other_edge = other_ref[:, 2 * STATIONS :].astype(F32)
    low = jnp.where(upper_core, other_edge, own_edge)
    high = jnp.where(upper_core, own_edge, other_edge)
    inner = jnp.where(lane < 16, low + pltpu.roll(high, LANES - 16, 1), 0.0)
    turned = jnp.where(lane < 8, pltpu.roll(inner, LANES - 8, 1), -pltpu.roll(inner, 8, 1))
    turned = jnp.where(lane < 16, turned, 0.0).astype(BF16)
    inner = inner.astype(BF16)
    real[...] = (
        own_ref[:, 0:STATIONS].astype(F32)
        + other_ref[:, 0:STATIONS].astype(F32)
        + lax.dot_general(inner, inner, contract, preferred_element_type=F32)
    )
    imag[...] = (
        own_ref[:, STATIONS : 2 * STATIONS].astype(F32)
        + other_ref[:, STATIONS : 2 * STATIONS].astype(F32)
        + lax.dot_general(turned, inner, contract, preferred_element_type=F32)
    )
    here = pl.ds(pl.multiple_of(place_ref[0] * count, count), count)
    across = pl.ds(pl.multiple_of(place_ref[1] * count, count), count)
    rows_ref[0] = real[here, :]
    rows_ref[1] = imag[here, :]
    send_ref[0:count, :] = real[across, :].astype(BF16)
    send_ref[count : 2 * count, :] = imag[across, :].astype(BF16)

    outer = jnp.where(second_chip, pltpu.roll(low, LANES - 16, 1), high)
    outer = jnp.where(lane < 16, outer, 0.0).T[0:16]
    edge_rows = outer[0:8] + pltpu.roll(outer[8:16], 4, 0)

    rows = lax.broadcasted_iota(jnp.int32, (STATIONS, STATIONS), 0)
    cols = lax.broadcasted_iota(jnp.int32, (STATIONS, STATIONS), 1)
    flag_real = jnp.where(rows == cols, 0.0, real[...]).astype(BF16)
    flag_real = jnp.concatenate([flag_real, outer.astype(BF16)], axis=0)
    flag_imag = jnp.where(rows == cols, 0.0, imag[...]).astype(BF16)
    width = STATIONS
    groups = cos_ref.shape[1] // width // 2
    for q in range(2 * groups):
        cosine = cos_ref[:, q * width : (q + 1) * width]
        sine = sin_ref[:, q * width : (q + 1) * width]
        by_cos = jnp.dot(flag_real, cosine, preferred_element_type=F32)
        by_sin = jnp.dot(flag_real, sine, preferred_element_type=F32)
        cross = jnp.dot(flag_imag, sine, preferred_element_type=F32)
        upper = by_cos[:STATIONS] + 2.0 * cross
        pixel = jnp.sum(
            cosine.astype(F32) * upper + sine.astype(F32) * by_sin[:STATIONS], axis=0, keepdims=True
        )
        first = by_cos[STATIONS : STATIONS + 8] - by_sin[STATIONS + 8 :]
        second = by_cos[STATIONS + 8 :] + by_sin[STATIONS : STATIONS + 8]
        beams = first + pltpu.roll(second, 4, 0)
        if q < groups:
            extra_ref[8 * q : 8 * q + 8, :] = beams
            extra_ref[8 * groups + 8 + q : 8 * groups + 9 + q, :] = pixel
        else:
            at = 2 * count + 8 * (q - groups)
            send_ref[at : at + 8, :] = beams.astype(BF16)
            at = 2 * count + 8 * groups + 8 + q - groups
            send_ref[at : at + 1, :] = pixel.astype(BF16)
    extra_ref[8 * groups : 8 * groups + 8, :] = edge_rows
    at = 2 * count + 8 * groups
    send_ref[at : at + 8, :] = edge_rows.astype(BF16)
    end = at + 8 + groups
    send_ref[end:, :] = jnp.zeros((send_ref.shape[0] - end, width), BF16)


def image_rows(place, own, other, cosine, sine, count):
    groups = cosine.shape[1] // 512
    return pl.pallas_call(
        image_kernel,
        out_shape=(
            jax.ShapeDtypeStruct((2, count, STATIONS), F32),
            jax.ShapeDtypeStruct((9 * groups + 8, STATIONS), F32),
            jax.ShapeDtypeStruct((2 * count + 8 * groups + 16, STATIONS), BF16),
        ),
        in_specs=[SMEM] + [VMEM] * 4,
        out_specs=(VMEM, VMEM, VMEM),
        scratch_shapes=[pltpu.VMEM((STATIONS, STATIONS), F32)] * 2,
        name="image_rows",
        **params(6 * 256 * 256 * 2048, 1 << 21),
    )(place, own, other, cosine, sine)


def finish_kernel(inv_total, image_scale, place_ref, rows_ref, extra_ref, got_ref, vis_ref, image_ref, turn):
    count = rows_ref.shape[1]
    groups = image_ref.shape[1] // STATIONS
    at = 8 * groups
    edge = extra_ref[at : at + 8, :] + got_ref[2 * count + at : 2 * count + at + 8, :].astype(F32)
    swapped = pltpu.roll(edge, 4, 0)
    low = lax.broadcasted_iota(jnp.int32, (8, STATIONS), 0) < 4
    swapped = jnp.where(low, swapped, -swapped)
    blank = jnp.zeros((LANES - 16, STATIONS), F32)
    turn[...] = jnp.concatenate([edge, swapped, blank], axis=0).T
    left = turn[pl.ds(pl.multiple_of(place_ref[0] * count, count), count), :]
    right = jnp.concatenate([edge, edge, blank], axis=0).astype(BF16)
    lane = lax.broadcasted_iota(jnp.int32, (count, LANES), 1)
    for part in range(2):
        got = got_ref[part * count : (part + 1) * count, :].astype(F32)
        chosen = jnp.where((lane < 8) if part == 0 else (lane >= 8), left, 0.0).astype(BF16)
        update = jnp.dot(chosen, right, preferred_element_type=F32)
        vis_ref[0, part] = (rows_ref[part] + got + update) * inv_total
    own_power = jnp.sum(jnp.sum(edge * edge, axis=1, keepdims=True), axis=0, keepdims=True)
    for q in range(groups):
        got = got_ref[2 * count + at + 8 + q : 2 * count + at + 9 + q, :].astype(F32)
        beams = extra_ref[8 * q : 8 * q + 8, :] + got_ref[
            2 * count + 8 * q : 2 * count + 8 * q + 8, :
        ].astype(F32)
        power = jnp.sum(beams * beams, axis=0, keepdims=True) - own_power
        image_ref[:, q * STATIONS : (q + 1) * STATIONS] = (
            extra_ref[at + 8 + q : at + 9 + q, :] + got + power
        ) * (inv_total * image_scale)


def finish(place, rows, extra, got, pixels, inv_total, image_scale):
    count = rows.shape[1]
    return pl.pallas_call(
        lambda *refs: finish_kernel(inv_total, image_scale, *refs),
        out_shape=(
            jax.ShapeDtypeStruct((1, 2, count, STATIONS), F32),
            jax.ShapeDtypeStruct((1, pixels), F32),
        ),
        in_specs=[SMEM] + [VMEM] * 3,
        out_specs=(VMEM, VMEM),
        scratch_shapes=[pltpu.VMEM((STATIONS, LANES), F32)],
        name="finish",
        **params(1 << 20, 1 << 18),
    )(place, rows, extra, got)


def on_device(voltages, fir_taps, station_of_slot, station_u, station_v, pixel_l, pixel_m):
    spec_dev = voltages.shape[1]
    pix_count = lax.axis_size("pix")
    spectra_total = spec_dev * pix_count
    pix = lax.axis_index("pix")
    across = jnp.where(pix < 2, pix + 2, pix - 2)
    place = jnp.stack([pix, across]).astype(jnp.int32)
    rows_l = pixel_l.shape[0] // pix_count
    sent = filter_bank(voltages, fir_taps).reshape(POINTS, ROWS // 2, 2, LANES)
    received = lax.all_to_all(sent, "chan", split_axis=0, concat_axis=0, tiled=True)

    block_l = jnp.concatenate(
        [
            lax.dynamic_slice_in_dim(pixel_l, pix * rows_l, rows_l, 0),
            lax.dynamic_slice_in_dim(pixel_l, across * rows_l, rows_l, 0),
            jnp.zeros((LANES - 2 * rows_l,), jnp.int32),
        ]
    )[None]
    pixels = rows_l * pixel_m.shape[0]
    cosine, sine = steering(
        lax.axis_index("chan")[None].astype(jnp.int32),
        station_u[None],
        station_v[None],
        block_l,
        jnp.concatenate([pixel_m, pixel_m])[None],
        2 * pixels,
    )
    station_row = station_of_slot.reshape(POINTS, 2).T.reshape(1, STATIONS)
    own = gram(place, received.reshape(-1, 2, LANES), station_row, cosine)
    other = lax.ppermute(own, "pix", [(0, 1), (1, 0), (2, 3), (3, 2)])
    rows, extra, send = image_rows(place, own, other, cosine, sine, STATIONS // pix_count)
    got = lax.ppermute(send, "pix", [(0, 2), (2, 0), (1, 3), (3, 1)])
    return finish(
        place, rows, extra, got, pixels, 1.0 / spectra_total, math.sqrt(spectra_total) / STATIONS
    )


def solution(mesh):
    in_specs = (P("chan", "pix", None), P(), P(), P(), P(), P(), P())
    out_specs = (P("chan", None, "pix", None), P("chan", "pix"))
    return jax.shard_map(
        on_device, mesh=mesh, in_specs=in_specs, out_specs=out_specs, check_vma=False
    )
```

```python
import math

import jax
import jax.numpy as jnp
import numpy as np
from jax import lax
from jax.experimental import pallas as pl
from jax.experimental.pallas import tpu as pltpu
from jax.sharding import PartitionSpec as P

POINTS = 128
TAPS = 4
GRID = 1024
LANES = 128
STATIONS = 256
EDGE = 8
ROWS = 18

VMEM = pl.BlockSpec(memory_space=pltpu.VMEM)
HBM = pl.BlockSpec(memory_space=pltpu.HBM)
ANY = pl.BlockSpec(memory_space=pl.ANY)
SMEM = pl.BlockSpec(memory_space=pltpu.SMEM)
F32 = jnp.float32
BF16 = jnp.bfloat16


def dft_matrix(points):
    counter = np.arange(points)
    angle = np.mod(counter[:, None] * counter[None, :], points) * (2.0 * math.pi / points)
    cosine, sine = np.cos(angle), np.sin(angle)
    table = np.block([[cosine, sine], [-sine, cosine]]) * points ** (-0.5)
    return jnp.asarray(table, dtype=F32).astype(BF16)


def params(flops, moved, limit=40 * 1024 * 1024):
    return dict(
        compiler_params=pltpu.CompilerParams(vmem_limit_bytes=limit),
        cost_estimate=pl.CostEstimate(flops=flops, bytes_accessed=moved, transcendentals=0),
    )


def filter_kernel(v_hbm, taps_hbm, dft_hbm, out_hbm, v_ref, taps_ref, dft_ref, ext, tail, wide, packed, sems):
    spec_dev = v_hbm.shape[1]
    copies = [pltpu.make_async_copy(v_hbm.at[s], v_ref.at[s], sems.at[s]) for s in range(2)]
    copies.append(pltpu.make_async_copy(dft_hbm, dft_ref, sems.at[2]))
    copies.append(pltpu.make_async_copy(taps_hbm, taps_ref, sems.at[3]))
    for i in (0, 3, 2, 1):
        copies[i].start()
    step = 256
    contract = (((1,), (1,)), ((), ()))
    for s in range(2):
        ext[s, 0:EDGE, :] = jnp.zeros((EDGE, 2 * POINTS), F32)
        ext[s, EDGE + spec_dev :, :] = jnp.zeros((EDGE, 2 * POINTS), F32)
    tail[2 * EDGE :, :] = jnp.zeros((LANES - 2 * EDGE, 2 * POINTS), BF16)

    copies[3].wait()
    taps = jnp.concatenate([taps_ref[...], taps_ref[...]], axis=1)

    def filtered(s, start, count):
        total = taps[0:1] * ext[s, EDGE + start : EDGE + start + count, :]
        for k in range(1, TAPS):
            total = total + taps[k : k + 1] * ext[s, EDGE - k + start : EDGE - k + start + count, :]
        return total

    for s in range(2):
        copies[s].wait()
        ext[s, EDGE : EDGE + spec_dev, :] = v_ref[s].astype(F32)
        if s == 0:
            copies[2].wait()
        for t in range(0, spec_dev, step):
            spectra = lax.dot_general(
                dft_ref[...], filtered(s, t, step).astype(BF16), contract, preferred_element_type=F32
            )
            for r in range(2):
                for part in range(step // LANES):
                    row = s * 8 + r * 4 + t // LANES + part
                    wide[pl.ds(row, POINTS, stride=ROWS), :] = spectra[
                        r * POINTS : (r + 1) * POINTS, part * LANES : (part + 1) * LANES
                    ]
    edges = jnp.concatenate([filtered(s, spec_dev, EDGE) for s in range(2)], axis=0)
    tail[0 : 2 * EDGE, :] = edges.astype(BF16)
    spectra = lax.dot_general(dft_ref[...], tail[...], contract, preferred_element_type=F32)
    for r in range(2):
        wide[pl.ds(16 + r, POINTS, stride=ROWS), :] = spectra[r * POINTS : (r + 1) * POINTS]
    chunk = POINTS * ROWS // 8
    writes = []
    for c in range(8):
        here = pl.ds(c * chunk // 2, chunk // 2)
        packed[here] = wide[c * chunk : (c + 1) * chunk, :].astype(BF16).reshape(chunk // 2, 2, LANES)
        writes.append(pltpu.make_async_copy(packed.at[here], out_hbm.at[here], sems.at[4 + c]))
        writes[-1].start()
    for write in writes:
        write.wait()


def filter_bank(voltages, fir_taps):
    pairs = POINTS * ROWS // 2
    return pl.pallas_call(
        filter_kernel,
        out_shape=jax.ShapeDtypeStruct((pairs, 2, LANES), BF16),
        in_specs=[HBM, HBM, HBM],
        out_specs=HBM,
        scratch_shapes=[
            pltpu.VMEM(voltages.shape, BF16),
            pltpu.VMEM(fir_taps.shape, F32),
            pltpu.VMEM((2 * POINTS, 2 * POINTS), BF16),
            pltpu.VMEM((2, 2 * EDGE + voltages.shape[1], 2 * POINTS), F32),
            pltpu.VMEM((LANES, 2 * POINTS), BF16),
            pltpu.VMEM((2 * pairs, LANES), F32),
            pltpu.VMEM((pairs, 2, LANES), BF16),
            pltpu.SemaphoreType.DMA((12,)),
        ],
        name="filter_bank",
        **params(2 * 256 * 256 * 1024, 1 << 20, 66_000_000),
    )(voltages, fir_taps, dft_matrix(POINTS))


def steering_kernel(chan_ref, u_ref, v_ref, l_ref, m_ref, cos_ref, sin_ref):
    freq = POINTS + chan_ref[0]
    rows = lax.broadcasted_iota(jnp.int32, (STATIONS, STATIONS), 0)
    cols = lax.broadcasted_iota(jnp.int32, (STATIONS, STATIONS), 1)
    eye = rows == cols

    def column(ref):
        return jnp.sum(jnp.where(eye, ref[...], 0), axis=1, keepdims=True)

    def phases(station, pixel):
        index = (freq * ((station * pixel) & (GRID - 1))) & (GRID - 1)
        angle = index.astype(F32) * (2.0 * math.pi / GRID)
        return jnp.cos(angle), jnp.sin(angle)

    l_cos, l_sin = phases(column(u_ref), l_ref[...])
    m_cos, m_sin = phases(column(v_ref), m_ref[...])
    first = lax.broadcasted_iota(jnp.int32, (STATIONS, LANES), 1) < 64
    for q in range(cos_ref.shape[1] // LANES):
        a_cos = jnp.where(first, l_cos[:, 2 * q : 2 * q + 1], l_cos[:, 2 * q + 1 : 2 * q + 2])
        a_sin = jnp.where(first, l_sin[:, 2 * q : 2 * q + 1], l_sin[:, 2 * q + 1 : 2 * q + 2])
        cos_ref[:, q * LANES : (q + 1) * LANES] = (a_cos * m_cos - a_sin * m_sin).astype(BF16)
        sin_ref[:, q * LANES : (q + 1) * LANES] = (a_sin * m_cos + a_cos * m_sin).astype(BF16)


def steering(channel, station_u, station_v, rows_l, pixel_m, pixels):
    out = jax.ShapeDtypeStruct((STATIONS, pixels), BF16)
    return pl.pallas_call(
        steering_kernel,
        out_shape=(out, out),
        in_specs=[SMEM] + [VMEM] * 4,
        out_specs=(VMEM, VMEM),
        name="steering",
        **params(6 * STATIONS * pixels, 4 * STATIONS * pixels),
    )(channel, station_u, station_v, rows_l, pixel_m)


def gram_kernel(recv_ref, station_ref, after_ref, out_ref, wide, slots):
    chunk = 256
    for c in range(0, POINTS * ROWS, chunk):
        wide[c : c + chunk, :] = recv_ref[c // 2 : (c + chunk) // 2].reshape(chunk, LANES).astype(F32)
    lane = lax.broadcasted_iota(jnp.int32, (POINTS, LANES), 1)
    head = lane < TAPS - 1
    edge = lane < EDGE
    left_out = jnp.logical_and(head, lax.axis_index("pix") > 0)

    def column(row):
        return wide[pl.ds(row, POINTS, stride=ROWS), :]

    for s in range(2):
        rows = slice(s * POINTS, (s + 1) * POINTS)
        for q in range(8):
            values = column(s * 8 + q)
            if q % 4 == 0:
                values = jnp.where(left_out, 0.0, values)
            slots[rows, q * LANES : (q + 1) * LANES] = values.astype(BF16)
        pieces = [
            pltpu.roll(column(16 + r), LANES - EDGE, 1) if s else column(16 + r) for r in range(2)
        ]
        pieces = [jnp.where(edge, piece, 0.0) for piece in pieces]
        pieces += [jnp.where(head, column(s * 8 + r * 4), 0.0) for r in range(2)]
        total = pieces[0]
        for i in range(1, 4):
            total = total + pltpu.roll(pieces[i], i * EDGE, 1)
        slots[rows, 8 * LANES :] = total.astype(BF16)
    rows = lax.broadcasted_iota(jnp.int32, (STATIONS, STATIONS), 0)
    select = jnp.where(rows == station_ref[...], 1.0, 0.0).astype(BF16)
    ordered = jnp.dot(select, slots[...], preferred_element_type=F32).astype(BF16)
    half = 4 * LANES
    spectra = ordered[:, : 2 * half]
    turned = jnp.concatenate([ordered[:, half : 2 * half], -ordered[:, :half]], axis=1)
    contract = (((1,), (1,)), ((), ()))
    real = lax.dot_general(spectra, spectra, contract, preferred_element_type=F32)
    imag = lax.dot_general(turned, spectra, contract, preferred_element_type=F32)
    out_ref[:, 0:STATIONS] = real.astype(BF16)
    out_ref[:, STATIONS : 2 * STATIONS] = imag.astype(BF16)
    out_ref[:, 2 * STATIONS :] = ordered[:, 2 * half :]


def gram(received, station_row, after):
    return pl.pallas_call(
        gram_kernel,
        out_shape=jax.ShapeDtypeStruct((STATIONS, 2 * STATIONS + LANES), BF16),
        in_specs=[VMEM, VMEM, ANY],
        out_specs=VMEM,
        scratch_shapes=[
            pltpu.VMEM((POINTS * ROWS, LANES), F32),
            pltpu.VMEM((STATIONS, 9 * LANES), BF16),
        ],
        name="gram",
        **params(6 * 256 * 256 * 1024, 1 << 20),
    )(received, station_row, after)


def image_kernel(own_ref, other_ref, cos_ref, sin_ref, rows_ref, extra_ref, send_ref, real, imag):
    count = rows_ref.shape[1]
    lane = lax.broadcasted_iota(jnp.int32, (STATIONS, LANES), 1)
    contract = (((1,), (1,)), ((), ()))
    pix = lax.axis_index("pix")
    upper_core = (pix & 1) == 1
    second_chip = pix >= 2
    own_edge = own_ref[:, 2 * STATIONS :].astype(F32)
    other_edge = other_ref[:, 2 * STATIONS :].astype(F32)
    low = jnp.where(upper_core, other_edge, own_edge)
    high = jnp.where(upper_core, own_edge, other_edge)
    inner = jnp.where(lane < 16, low + pltpu.roll(high, LANES - 16, 1), 0.0)
    turned = jnp.where(lane < 8, pltpu.roll(inner, LANES - 8, 1), -pltpu.roll(inner, 8, 1))
    turned = jnp.where(lane < 16, turned, 0.0).astype(BF16)
    inner = inner.astype(BF16)
    real[...] = (
        own_ref[:, 0:STATIONS].astype(F32)
        + other_ref[:, 0:STATIONS].astype(F32)
        + lax.dot_general(inner, inner, contract, preferred_element_type=F32)
    )
    imag[...] = (
        own_ref[:, STATIONS : 2 * STATIONS].astype(F32)
        + other_ref[:, STATIONS : 2 * STATIONS].astype(F32)
        + lax.dot_general(turned, inner, contract, preferred_element_type=F32)
    )
    here = pl.ds(pl.multiple_of(pix * count, count), count)
    across = pl.ds(pl.multiple_of((pix ^ 2) * count, count), count)
    rows_ref[0] = real[here, :]
    rows_ref[1] = imag[here, :]
    send_ref[0:count, :] = real[across, :].astype(BF16)
    send_ref[count : 2 * count, :] = imag[across, :].astype(BF16)

    outer = jnp.where(second_chip, pltpu.roll(low, LANES - 16, 1), high)
    outer = jnp.where(lane < 16, outer, 0.0).T[0:16]
    edge_rows = outer[0:8] + pltpu.roll(outer[8:16], 4, 0)

    rows = lax.broadcasted_iota(jnp.int32, (STATIONS, STATIONS), 0)
    cols = lax.broadcasted_iota(jnp.int32, (STATIONS, STATIONS), 1)
    flag_real = jnp.where(rows == cols, 0.0, real[...]).astype(BF16)
    flag_real = jnp.concatenate([flag_real, outer.astype(BF16)], axis=0)
    flag_imag = jnp.where(rows == cols, 0.0, imag[...]).astype(BF16)
    width = STATIONS
    groups = cos_ref.shape[1] // width // 2
    for q in range(2 * groups):
        cosine = cos_ref[:, q * width : (q + 1) * width]
        sine = sin_ref[:, q * width : (q + 1) * width]
        by_cos = jnp.dot(flag_real, cosine, preferred_element_type=F32)
        by_sin = jnp.dot(flag_real, sine, preferred_element_type=F32)
        cross = jnp.dot(flag_imag, sine, preferred_element_type=F32)
        upper = by_cos[:STATIONS] + 2.0 * cross
        pixel = jnp.sum(
            cosine.astype(F32) * upper + sine.astype(F32) * by_sin[:STATIONS], axis=0, keepdims=True
        )
        first = by_cos[STATIONS : STATIONS + 8] - by_sin[STATIONS + 8 :]
        second = by_cos[STATIONS + 8 :] + by_sin[STATIONS : STATIONS + 8]
        beams = first + pltpu.roll(second, 4, 0)
        if q < groups:
            extra_ref[8 * q : 8 * q + 8, :] = beams
            extra_ref[8 * groups + 8 + q : 8 * groups + 9 + q, :] = pixel
        else:
            at = 2 * count + 8 * (q - groups)
            send_ref[at : at + 8, :] = beams.astype(BF16)
            at = 2 * count + 8 * groups + 8 + q - groups
            send_ref[at : at + 1, :] = pixel.astype(BF16)
    extra_ref[8 * groups : 8 * groups + 8, :] = edge_rows
    at = 2 * count + 8 * groups
    send_ref[at : at + 8, :] = edge_rows.astype(BF16)
    end = at + 8 + groups
    send_ref[end:, :] = jnp.zeros((send_ref.shape[0] - end, width), BF16)


def image_rows(own, other, cosine, sine, count):
    groups = cosine.shape[1] // 512
    return pl.pallas_call(
        image_kernel,
        out_shape=(
            jax.ShapeDtypeStruct((2, count, STATIONS), F32),
            jax.ShapeDtypeStruct((9 * groups + 8, STATIONS), F32),
            jax.ShapeDtypeStruct((2 * count + 8 * groups + 16, STATIONS), BF16),
        ),
        in_specs=[VMEM] * 4,
        out_specs=(VMEM, VMEM, VMEM),
        scratch_shapes=[pltpu.VMEM((STATIONS, STATIONS), F32)] * 2,
        name="image_rows",
        **params(6 * 256 * 256 * 2048, 1 << 21),
    )(own, other, cosine, sine)


def finish_kernel(inv_total, image_scale, rows_ref, extra_ref, got_ref, vis_ref, image_ref, turn):
    pix = lax.axis_index("pix")
    count = rows_ref.shape[1]
    groups = image_ref.shape[1] // STATIONS
    at = 8 * groups
    edge = extra_ref[at : at + 8, :] + got_ref[2 * count + at : 2 * count + at + 8, :].astype(F32)
    swapped = pltpu.roll(edge, 4, 0)
    low = lax.broadcasted_iota(jnp.int32, (8, STATIONS), 0) < 4
    swapped = jnp.where(low, swapped, -swapped)
    blank = jnp.zeros((LANES - 16, STATIONS), F32)
    turn[...] = jnp.concatenate([edge, swapped, blank], axis=0).T
    left = turn[pl.ds(pl.multiple_of(pix * count, count), count), :]
    right = jnp.concatenate([edge, edge, blank], axis=0).astype(BF16)
    lane = lax.broadcasted_iota(jnp.int32, (count, LANES), 1)
    for part in range(2):
        got = got_ref[part * count : (part + 1) * count, :].astype(F32)
        chosen = jnp.where((lane < 8) if part == 0 else (lane >= 8), left, 0.0).astype(BF16)
        update = jnp.dot(chosen, right, preferred_element_type=F32)
        vis_ref[0, part] = (rows_ref[part] + got + update) * inv_total
    own_power = jnp.sum(jnp.sum(edge * edge, axis=1, keepdims=True), axis=0, keepdims=True)
    for q in range(groups):
        got = got_ref[2 * count + at + 8 + q : 2 * count + at + 9 + q, :].astype(F32)
        beams = extra_ref[8 * q : 8 * q + 8, :] + got_ref[
            2 * count + 8 * q : 2 * count + 8 * q + 8, :
        ].astype(F32)
        power = jnp.sum(beams * beams, axis=0, keepdims=True) - own_power
        image_ref[:, q * STATIONS : (q + 1) * STATIONS] = (
            extra_ref[at + 8 + q : at + 9 + q, :] + got + power
        ) * (inv_total * image_scale)


def finish(rows, extra, got, pixels, inv_total, image_scale):
    count = rows.shape[1]
    return pl.pallas_call(
        lambda *refs: finish_kernel(inv_total, image_scale, *refs),
        out_shape=(
            jax.ShapeDtypeStruct((1, 2, count, STATIONS), F32),
            jax.ShapeDtypeStruct((1, pixels), F32),
        ),
        in_specs=[VMEM] * 3,
        out_specs=(VMEM, VMEM),
        scratch_shapes=[pltpu.VMEM((STATIONS, LANES), F32)],
        name="finish",
        **params(1 << 20, 1 << 18),
    )(rows, extra, got)


def on_device(voltages, fir_taps, station_of_slot, station_u, station_v, pixel_l, pixel_m):
    spec_dev = voltages.shape[1]
    pix_count = lax.axis_size("pix")
    spectra_total = spec_dev * pix_count
    pix = lax.axis_index("pix")
    across = jnp.where(pix < 2, pix + 2, pix - 2)
    rows_l = pixel_l.shape[0] // pix_count
    sent = filter_bank(voltages, fir_taps).reshape(POINTS, ROWS // 2, 2, LANES)
    received = lax.all_to_all(sent, "chan", split_axis=0, concat_axis=0, tiled=True)

    block_l = jnp.concatenate(
        [
            lax.dynamic_slice_in_dim(pixel_l, pix * rows_l, rows_l, 0),
            lax.dynamic_slice_in_dim(pixel_l, across * rows_l, rows_l, 0),
            jnp.zeros((LANES - 2 * rows_l,), jnp.int32),
        ]
    )[None]
    pixels = rows_l * pixel_m.shape[0]
    cosine, sine = steering(
        lax.axis_index("chan")[None].astype(jnp.int32),
        station_u[None],
        station_v[None],
        block_l,
        jnp.concatenate([pixel_m, pixel_m])[None],
        2 * pixels,
    )
    station_row = station_of_slot.reshape(POINTS, 2).T.reshape(1, STATIONS)
    own = gram(received.reshape(-1, 2, LANES), station_row, cosine)
    other = lax.ppermute(own, "pix", [(0, 1), (1, 0), (2, 3), (3, 2)])
    rows, extra, send = image_rows(own, other, cosine, sine, STATIONS // pix_count)
    got = lax.ppermute(send, "pix", [(0, 2), (2, 0), (1, 3), (3, 1)])
    return finish(rows, extra, got, pixels, 1.0 / spectra_total, math.sqrt(spectra_total) / STATIONS)


def solution(mesh):
    in_specs = (P("chan", "pix", None), P(), P(), P(), P(), P(), P())
    out_specs = (P("chan", None, "pix", None), P("chan", "pix"))
    return jax.shard_map(
        on_device, mesh=mesh, in_specs=in_specs, out_specs=out_specs, check_vma=False
    )
```

```python
import math

import jax
import jax.numpy as jnp
import numpy as np
from jax import lax
from jax.experimental import pallas as pl
from jax.experimental.pallas import tpu as pltpu
from jax.sharding import PartitionSpec as P

POINTS = 128
TAPS = 4
GRID = 1024
LANES = 128
STATIONS = 256
EDGE = 8
ROWS = 18

VMEM = pl.BlockSpec(memory_space=pltpu.VMEM)
HBM = pl.BlockSpec(memory_space=pltpu.HBM)
ANY = pl.BlockSpec(memory_space=pl.ANY)
SMEM = pl.BlockSpec(memory_space=pltpu.SMEM)
F32 = jnp.float32
BF16 = jnp.bfloat16


def dft_matrix(points):
    counter = np.arange(points)
    angle = np.mod(counter[:, None] * counter[None, :], points) * (2.0 * math.pi / points)
    cosine, sine = np.cos(angle), np.sin(angle)
    table = np.block([[cosine, sine], [-sine, cosine]]) * points ** (-0.5)
    return jnp.asarray(table, dtype=F32).astype(BF16)


def params(flops, moved, limit=40 * 1024 * 1024):
    return dict(
        compiler_params=pltpu.CompilerParams(vmem_limit_bytes=limit),
        cost_estimate=pl.CostEstimate(flops=flops, bytes_accessed=moved, transcendentals=0),
    )


def filter_kernel(v_hbm, taps_hbm, dft_hbm, out_hbm, v_ref, taps_ref, dft_ref, ext, tail, wide, packed, sems):
    spec_dev = v_hbm.shape[1]
    step = 256
    pieces = [(s, t) for s in range(2) for t in range(0, spec_dev, step)]
    copies = [pltpu.make_async_copy(v_hbm.at[s], v_ref.at[s], sems.at[s]) for s in range(2)]
    copies.append(pltpu.make_async_copy(taps_hbm, taps_ref, sems.at[2]))
    copies.append(pltpu.make_async_copy(dft_hbm, dft_ref, sems.at[3]))
    for i in (2, 0, 3, 1):
        copies[i].start()
    contract = (((1,), (1,)), ((), ()))
    blank = jnp.zeros((EDGE, POINTS), F32)
    for s in range(2):
        for half in range(2):
            ext[s, half, 0:EDGE, :] = blank
            ext[s, half, EDGE + spec_dev :, :] = blank
    tail[2 * EDGE :, :] = jnp.zeros((LANES - 2 * EDGE, 2 * POINTS), BF16)
    copies[2].wait()
    taps = taps_ref[...]

    def filtered(s, start, count):
        halves = []
        for half in range(2):
            total = taps[0:1] * ext[s, half, EDGE + start : EDGE + start + count, :]
            for k in range(1, TAPS):
                first = EDGE - k + start
                total = total + taps[k : k + 1] * ext[s, half, first : first + count, :]
            halves.append(total.astype(BF16))
        return jnp.concatenate(halves, axis=1)

    for i, (s, t) in enumerate(pieces):
        if t == 0:
            copies[s].wait()
            for half in range(2):
                ext[s, half, EDGE : EDGE + spec_dev, :] = v_ref[
                    s, :, half * POINTS : (half + 1) * POINTS
                ].astype(F32)
        if i == 0:
            copies[3].wait()
        spectra = lax.dot_general(
            dft_ref[...], filtered(s, t, step), contract, preferred_element_type=F32
        )
        for r in range(2):
            for part in range(step // LANES):
                row = s * 8 + r * 4 + t // LANES + part
                wide[pl.ds(row, POINTS, stride=ROWS), :] = spectra[
                    r * POINTS : (r + 1) * POINTS, part * LANES : (part + 1) * LANES
                ]
    tail[0 : 2 * EDGE, :] = jnp.concatenate([filtered(s, spec_dev, EDGE) for s in range(2)], axis=0)
    spectra = lax.dot_general(dft_ref[...], tail[...], contract, preferred_element_type=F32)
    for r in range(2):
        wide[pl.ds(16 + r, POINTS, stride=ROWS), :] = spectra[r * POINTS : (r + 1) * POINTS]
    chunk = POINTS * ROWS // 8
    writes = []
    for c in range(8):
        here = pl.ds(c * chunk, chunk)
        packed[here] = wide[c * chunk : (c + 1) * chunk, :].astype(BF16)
        writes.append(pltpu.make_async_copy(packed.at[here], out_hbm.at[here], sems.at[4 + c]))
        writes[-1].start()
    for write in writes:
        write.wait()


def filter_bank(voltages, fir_taps):
    rows = POINTS * ROWS
    return pl.pallas_call(
        filter_kernel,
        out_shape=jax.ShapeDtypeStruct((rows, LANES), BF16),
        in_specs=[HBM, HBM, HBM],
        out_specs=HBM,
        scratch_shapes=[
            pltpu.VMEM(voltages.shape, BF16),
            pltpu.VMEM(fir_taps.shape, F32),
            pltpu.VMEM((2 * POINTS, 2 * POINTS), BF16),
            pltpu.VMEM((2, 2, 2 * EDGE + voltages.shape[1], POINTS), F32),
            pltpu.VMEM((LANES, 2 * POINTS), BF16),
            pltpu.VMEM((rows, LANES), F32),
            pltpu.VMEM((rows, LANES), BF16),
            pltpu.SemaphoreType.DMA((12,)),
        ],
        name="filter_bank",
        **params(2 * 256 * 256 * 1024, 1 << 20, 66_000_000),
    )(voltages, fir_taps, dft_matrix(POINTS))


def steering_kernel(chan_ref, u_ref, v_ref, l_ref, m_ref, *out_refs):
    freq = POINTS + chan_ref[0]
    rows = lax.broadcasted_iota(jnp.int32, (STATIONS, STATIONS), 0)
    cols = lax.broadcasted_iota(jnp.int32, (STATIONS, STATIONS), 1)
    eye = rows == cols

    def column(ref):
        return jnp.sum(jnp.where(eye, ref[...], 0), axis=1, keepdims=True)

    def phases(station, pixel):
        index = (freq * ((station * pixel) & (GRID - 1))) & (GRID - 1)
        angle = index.astype(F32) * (2.0 * math.pi / GRID)
        return jnp.cos(angle), jnp.sin(angle)

    l_cos, l_sin = phases(column(u_ref), l_ref[...])
    m_cos, m_sin = phases(column(v_ref), m_ref[...])
    first = lax.broadcasted_iota(jnp.int32, (STATIONS, LANES), 1) < 64
    blocks = out_refs[0].shape[1] // LANES
    for q in range(2 * blocks):
        cos_ref, sin_ref = out_refs[2 * (q // blocks) : 2 * (q // blocks) + 2]
        at = q % blocks * LANES
        a_cos = jnp.where(first, l_cos[:, 2 * q : 2 * q + 1], l_cos[:, 2 * q + 1 : 2 * q + 2])
        a_sin = jnp.where(first, l_sin[:, 2 * q : 2 * q + 1], l_sin[:, 2 * q + 1 : 2 * q + 2])
        cos_ref[:, at : at + LANES] = (a_cos * m_cos - a_sin * m_sin).astype(BF16)
        sin_ref[:, at : at + LANES] = (a_sin * m_cos + a_cos * m_sin).astype(BF16)


def steering(channel, station_u, station_v, rows_l, pixel_m, pixels):
    out = jax.ShapeDtypeStruct((STATIONS, pixels), BF16)
    return pl.pallas_call(
        steering_kernel,
        out_shape=(out,) * 4,
        in_specs=[SMEM] + [VMEM] * 4,
        out_specs=(VMEM,) * 4,
        name="steering",
        **params(12 * STATIONS * pixels, 8 * STATIONS * pixels),
    )(channel, station_u, station_v, rows_l, pixel_m)


def gram_kernel(recv_ref, station_ref, after_ref, out_ref, wide, slots):
    chunk = 256
    for c in range(0, POINTS * ROWS, chunk):
        wide[c : c + chunk, :] = recv_ref[c : c + chunk].astype(F32)
    lane = lax.broadcasted_iota(jnp.int32, (POINTS, LANES), 1)
    head = lane < TAPS - 1
    edge = lane < EDGE
    left_out = jnp.logical_and(head, lax.axis_index("pix") > 0)

    def column(row):
        return wide[pl.ds(row, POINTS, stride=ROWS), :]

    for s in range(2):
        rows = slice(s * POINTS, (s + 1) * POINTS)
        for q in range(8):
            values = column(s * 8 + q)
            if q % 4 == 0:
                values = jnp.where(left_out, 0.0, values)
            slots[rows, q * LANES : (q + 1) * LANES] = values.astype(BF16)
        pieces = [
            pltpu.roll(column(16 + r), LANES - EDGE, 1) if s else column(16 + r) for r in range(2)
        ]
        pieces = [jnp.where(edge, piece, 0.0) for piece in pieces]
        pieces += [jnp.where(head, column(s * 8 + r * 4), 0.0) for r in range(2)]
        total = pieces[0]
        for i in range(1, 4):
            total = total + pltpu.roll(pieces[i], i * EDGE, 1)
        slots[rows, 8 * LANES :] = total.astype(BF16)
    rows = lax.broadcasted_iota(jnp.int32, (STATIONS, STATIONS), 0)
    select = jnp.where(rows == station_ref[...], 1.0, 0.0).astype(BF16)
    ordered = jnp.dot(select, slots[...], preferred_element_type=F32).astype(BF16)
    half = 4 * LANES
    spectra = ordered[:, : 2 * half]
    turned = jnp.concatenate([ordered[:, half : 2 * half], -ordered[:, :half]], axis=1)
    contract = (((1,), (1,)), ((), ()))
    real = lax.dot_general(spectra, spectra, contract, preferred_element_type=F32)
    imag = lax.dot_general(turned, spectra, contract, preferred_element_type=F32)
    out_ref[:, 0:STATIONS] = real.astype(BF16)
    out_ref[:, STATIONS : 2 * STATIONS] = imag.astype(BF16)
    out_ref[:, 2 * STATIONS :] = ordered[:, 2 * half :]


def gram(received, station_row, after):
    return pl.pallas_call(
        gram_kernel,
        out_shape=jax.ShapeDtypeStruct((STATIONS, 2 * STATIONS + LANES), BF16),
        in_specs=[VMEM, VMEM, ANY],
        out_specs=VMEM,
        scratch_shapes=[
            pltpu.VMEM((POINTS * ROWS, LANES), F32),
            pltpu.VMEM((STATIONS, 9 * LANES), BF16),
        ],
        name="gram",
        **params(6 * 256 * 256 * 1024, 1 << 20),
    )(received, station_row, after)


def chip_sums(own_ref, other_ref, real, imag):
    pix = lax.axis_index("pix")
    lane = lax.broadcasted_iota(jnp.int32, (STATIONS, LANES), 1)
    contract = (((1,), (1,)), ((), ()))
    upper_core = (pix & 1) == 1
    own_edge = own_ref[:, 2 * STATIONS :].astype(F32)
    other_edge = other_ref[:, 2 * STATIONS :].astype(F32)
    low = jnp.where(upper_core, other_edge, own_edge)
    high = jnp.where(upper_core, own_edge, other_edge)
    outer = jnp.where(pix >= 2, pltpu.roll(low, LANES - 16, 1), high)
    outer = jnp.where(lane < 16, outer, 0.0).T[0:16]
    inner = jnp.where(lane < 16, low + pltpu.roll(high, LANES - 16, 1), 0.0)
    turned = jnp.where(lane < 8, pltpu.roll(inner, LANES - 8, 1), -pltpu.roll(inner, 8, 1))
    turned = jnp.where(lane < 16, turned, 0.0).astype(BF16)
    inner = inner.astype(BF16)
    real[...] = (
        own_ref[:, 0:STATIONS].astype(F32)
        + other_ref[:, 0:STATIONS].astype(F32)
        + lax.dot_general(inner, inner, contract, preferred_element_type=F32)
    )
    imag[...] = (
        own_ref[:, STATIONS : 2 * STATIONS].astype(F32)
        + other_ref[:, STATIONS : 2 * STATIONS].astype(F32)
        + lax.dot_general(turned, inner, contract, preferred_element_type=F32)
    )
    return outer


def partial_image(real, imag, outer, cos_ref, sin_ref, store):
    rows = lax.broadcasted_iota(jnp.int32, (STATIONS, STATIONS), 0)
    cols = lax.broadcasted_iota(jnp.int32, (STATIONS, STATIONS), 1)
    flag_real = jnp.where(rows == cols, 0.0, real[...]).astype(BF16)
    flag_real = jnp.concatenate([flag_real, outer.astype(BF16)], axis=0)
    flag_imag = jnp.where(rows == cols, 0.0, imag[...]).astype(BF16)
    width = STATIONS
    for q in range(cos_ref.shape[1] // width):
        cosine = cos_ref[:, q * width : (q + 1) * width]
        sine = sin_ref[:, q * width : (q + 1) * width]
        by_cos = jnp.dot(flag_real, cosine, preferred_element_type=F32)
        by_sin = jnp.dot(flag_real, sine, preferred_element_type=F32)
        cross = jnp.dot(flag_imag, sine, preferred_element_type=F32)
        upper = by_cos[:STATIONS] + 2.0 * cross
        pixel = jnp.sum(
            cosine.astype(F32) * upper + sine.astype(F32) * by_sin[:STATIONS], axis=0, keepdims=True
        )
        first = by_cos[STATIONS : STATIONS + 8] - by_sin[STATIONS + 8 :]
        second = by_cos[STATIONS + 8 :] + by_sin[STATIONS : STATIONS + 8]
        store(q, first + pltpu.roll(second, 4, 0), pixel)


def send_kernel(own_ref, other_ref, cos_ref, sin_ref, send_ref, real, imag):
    groups = cos_ref.shape[1] // STATIONS
    count = STATIONS // 4
    outer = chip_sums(own_ref, other_ref, real, imag)
    across = pl.ds(pl.multiple_of((lax.axis_index("pix") ^ 2) * count, count), count)
    send_ref[0:count, :] = real[across, :].astype(BF16)
    send_ref[count : 2 * count, :] = imag[across, :].astype(BF16)
    base = 2 * count
    edge = base + 8 * groups
    send_ref[edge : edge + 8, :] = (outer[0:8] + pltpu.roll(outer[8:16], 4, 0)).astype(BF16)
    send_ref[edge + 8 :, :] = jnp.zeros((send_ref.shape[0] - edge - 8, STATIONS), BF16)

    def store(q, beams, pixel):
        send_ref[base + 8 * q : base + 8 * q + 8, :] = beams.astype(BF16)
        send_ref[edge + 8 + q : edge + 9 + q, :] = pixel.astype(BF16)

    partial_image(real, imag, outer, cos_ref, sin_ref, store)


def keep_kernel(own_ref, other_ref, cos_ref, sin_ref, after_ref, rows_ref, extra_ref, real, imag):
    groups = cos_ref.shape[1] // STATIONS
    count = rows_ref.shape[1]
    outer = chip_sums(own_ref, other_ref, real, imag)
    here = pl.ds(pl.multiple_of(lax.axis_index("pix") * count, count), count)
    rows_ref[0] = real[here, :]
    rows_ref[1] = imag[here, :]
    edge = 8 * groups
    extra_ref[edge : edge + 8, :] = outer[0:8] + pltpu.roll(outer[8:16], 4, 0)

    def store(q, beams, pixel):
        extra_ref[8 * q : 8 * q + 8, :] = beams
        extra_ref[edge + 8 + q : edge + 9 + q, :] = pixel

    partial_image(real, imag, outer, cos_ref, sin_ref, store)


def send_part(own, other, cosine, sine, count):
    groups = cosine.shape[1] // STATIONS
    return pl.pallas_call(
        send_kernel,
        out_shape=jax.ShapeDtypeStruct((2 * count + 8 * groups + 16, STATIONS), BF16),
        in_specs=[VMEM] * 4,
        out_specs=VMEM,
        scratch_shapes=[pltpu.VMEM((STATIONS, STATIONS), F32)] * 2,
        name="send_part",
        **params(6 * 256 * 256 * 1024, 1 << 20),
    )(own, other, cosine, sine)


def keep_part(own, other, cosine, sine, after, count):
    groups = cosine.shape[1] // STATIONS
    return pl.pallas_call(
        keep_kernel,
        out_shape=(
            jax.ShapeDtypeStruct((2, count, STATIONS), F32),
            jax.ShapeDtypeStruct((9 * groups + 8, STATIONS), F32),
        ),
        in_specs=[VMEM] * 4 + [ANY],
        out_specs=(VMEM, VMEM),
        scratch_shapes=[pltpu.VMEM((STATIONS, STATIONS), F32)] * 2,
        name="keep_part",
        **params(6 * 256 * 256 * 1024, 1 << 20),
    )(own, other, cosine, sine, after)


def finish_kernel(inv_total, image_scale, rows_ref, extra_ref, got_ref, vis_ref, image_ref, turn):
    pix = lax.axis_index("pix")
    count = rows_ref.shape[1]
    groups = image_ref.shape[1] // STATIONS
    at = 8 * groups
    edge = extra_ref[at : at + 8, :] + got_ref[2 * count + at : 2 * count + at + 8, :].astype(F32)
    swapped = pltpu.roll(edge, 4, 0)
    low = lax.broadcasted_iota(jnp.int32, (8, STATIONS), 0) < 4
    turn[...] = jnp.concatenate([edge, jnp.where(low, swapped, -swapped)], axis=0).T
    left = turn[pl.ds(pl.multiple_of(pix * count, count), count), :]
    right = jnp.concatenate([edge, edge], axis=0).astype(BF16)
    lane = lax.broadcasted_iota(jnp.int32, left.shape, 1)
    for part in range(2):
        got = got_ref[part * count : (part + 1) * count, :].astype(F32)
        chosen = jnp.where((lane < 8) if part == 0 else (lane >= 8), left, 0.0).astype(BF16)
        update = jnp.dot(chosen, right, preferred_element_type=F32)
        vis_ref[0, part] = (rows_ref[part] + got + update) * inv_total
    own_power = jnp.sum(jnp.sum(edge * edge, axis=1, keepdims=True), axis=0, keepdims=True)
    for q in range(groups):
        got = got_ref[2 * count + at + 8 + q : 2 * count + at + 9 + q, :].astype(F32)
        beams = extra_ref[8 * q : 8 * q + 8, :] + got_ref[
            2 * count + 8 * q : 2 * count + 8 * q + 8, :
        ].astype(F32)
        power = jnp.sum(beams * beams, axis=0, keepdims=True) - own_power
        image_ref[:, q * STATIONS : (q + 1) * STATIONS] = (
            extra_ref[at + 8 + q : at + 9 + q, :] + got + power
        ) * (inv_total * image_scale)


def finish(rows, extra, got, pixels, inv_total, image_scale):
    count = rows.shape[1]
    return pl.pallas_call(
        lambda *refs: finish_kernel(inv_total, image_scale, *refs),
        out_shape=(
            jax.ShapeDtypeStruct((1, 2, count, STATIONS), F32),
            jax.ShapeDtypeStruct((1, pixels), F32),
        ),
        in_specs=[VMEM] * 3,
        out_specs=(VMEM, VMEM),
        scratch_shapes=[pltpu.VMEM((STATIONS, 16), F32)],
        name="finish",
        **params(1 << 20, 1 << 18),
    )(rows, extra, got)


def on_device(voltages, fir_taps, station_of_slot, station_u, station_v, pixel_l, pixel_m):
    spec_dev = voltages.shape[1]
    pix_count = lax.axis_size("pix")
    spectra_total = spec_dev * pix_count
    pix = lax.axis_index("pix")
    across = jnp.where(pix < 2, pix + 2, pix - 2)
    rows_l = pixel_l.shape[0] // pix_count
    sent = filter_bank(voltages, fir_taps).reshape(POINTS, ROWS // 2, 2, LANES)
    received = lax.all_to_all(sent, "chan", split_axis=0, concat_axis=0, tiled=True)

    block_l = jnp.concatenate(
        [
            lax.dynamic_slice_in_dim(pixel_l, pix * rows_l, rows_l, 0),
            lax.dynamic_slice_in_dim(pixel_l, across * rows_l, rows_l, 0),
            jnp.zeros((LANES - 2 * rows_l,), jnp.int32),
        ]
    )[None]
    pixels = rows_l * pixel_m.shape[0]
    here_cos, here_sin, across_cos, across_sin = steering(
        lax.axis_index("chan")[None].astype(jnp.int32),
        station_u[None],
        station_v[None],
        block_l,
        jnp.concatenate([pixel_m, pixel_m])[None],
        pixels,
    )
    station_row = station_of_slot.reshape(POINTS, 2).T.reshape(1, STATIONS)
    own = gram(received.reshape(-1, LANES), station_row, here_cos)
    other = lax.ppermute(own, "pix", [(0, 1), (1, 0), (2, 3), (3, 2)])
    count = STATIONS // pix_count
    send = send_part(own, other, across_cos, across_sin, count)
    got = lax.ppermute(send, "pix", [(0, 2), (2, 0), (1, 3), (3, 1)])
    rows, extra = keep_part(own, other, here_cos, here_sin, send, count)
    return finish(rows, extra, got, pixels, 1.0 / spectra_total, math.sqrt(spectra_total) / STATIONS)


def solution(mesh):
    in_specs = (P("chan", "pix", None), P(), P(), P(), P(), P(), P())
    out_specs = (P("chan", None, "pix", None), P("chan", "pix"))
    return jax.shard_map(
        on_device, mesh=mesh, in_specs=in_specs, out_specs=out_specs, check_vma=False
    )
```

```python
import math

import jax
import jax.numpy as jnp
import numpy as np
from jax import lax
from jax.experimental import pallas as pl
from jax.experimental.pallas import tpu as pltpu
from jax.sharding import PartitionSpec as P

POINTS = 128
TAPS = 4
GRID = 1024
LANES = 128
STATIONS = 256
BACKWARDS = list(range(POINTS))[::-1]
EDGE = 8
ROWS = 18

VMEM = pl.BlockSpec(memory_space=pltpu.VMEM)
HBM = pl.BlockSpec(memory_space=pltpu.HBM)
ANY = pl.BlockSpec(memory_space=pl.ANY)
SMEM = pl.BlockSpec(memory_space=pltpu.SMEM)
F32 = jnp.float32
BF16 = jnp.bfloat16


def dft_matrix(points):
    counter = np.arange(points)
    angle = np.mod(counter[:, None] * counter[None, :], points) * (2.0 * math.pi / points)
    cosine, sine = np.cos(angle), np.sin(angle)
    table = np.block([[cosine, sine], [-sine, cosine]]) * points ** (-0.5)
    table = table.reshape(2, points, 2 * points)[:, ::-1].reshape(2 * points, 2 * points)
    return jnp.asarray(table, dtype=F32).astype(BF16)


def params(flops, moved, limit=40 * 1024 * 1024):
    return dict(
        compiler_params=pltpu.CompilerParams(vmem_limit_bytes=limit),
        cost_estimate=pl.CostEstimate(flops=flops, bytes_accessed=moved, transcendentals=0),
    )


def filter_kernel(v_hbm, taps_hbm, dft_hbm, out_hbm, v_ref, taps_ref, dft_ref, ext, tail, wide, packed, sems):
    spec_dev = v_hbm.shape[1]
    step = 256
    pieces = [(s, t) for s in range(2) for t in range(0, spec_dev, step)]
    copies = [pltpu.make_async_copy(v_hbm.at[s], v_ref.at[s], sems.at[s]) for s in range(2)]
    copies.append(pltpu.make_async_copy(taps_hbm, taps_ref, sems.at[2]))
    copies.append(pltpu.make_async_copy(dft_hbm, dft_ref, sems.at[3]))
    for i in (2, 0, 3, 1):
        copies[i].start()
    contract = (((1,), (1,)), ((), ()))
    blank = jnp.zeros((EDGE, POINTS), F32)
    for s in range(2):
        for half in range(2):
            ext[s, half, 0:EDGE, :] = blank
            ext[s, half, EDGE + spec_dev :, :] = blank
    tail[2 * EDGE :, :] = jnp.zeros((LANES - 2 * EDGE, 2 * POINTS), BF16)
    copies[2].wait()
    taps = taps_ref[...]

    def filtered(s, start, count):
        halves = []
        for half in range(2):
            total = taps[0:1] * ext[s, half, EDGE + start : EDGE + start + count, :]
            for k in range(1, TAPS):
                first = EDGE - k + start
                total = total + taps[k : k + 1] * ext[s, half, first : first + count, :]
            halves.append(total.astype(BF16))
        return jnp.concatenate(halves, axis=1)

    for i, (s, t) in enumerate(pieces):
        if t == 0:
            copies[s].wait()
            for half in range(2):
                ext[s, half, EDGE : EDGE + spec_dev, :] = v_ref[
                    s, :, half * POINTS : (half + 1) * POINTS
                ].astype(F32)
        if i == 0:
            copies[3].wait()
        spectra = lax.dot_general(
            dft_ref[...], filtered(s, t, step), contract, preferred_element_type=F32
        )
        for r in range(2):
            for part in range(step // LANES):
                row = s * 8 + r * 4 + t // LANES + part
                wide[pl.ds(row, POINTS, stride=ROWS), :] = spectra[
                    r * POINTS : (r + 1) * POINTS, part * LANES : (part + 1) * LANES
                ]
    tail[0 : 2 * EDGE, :] = jnp.concatenate([filtered(s, spec_dev, EDGE) for s in range(2)], axis=0)
    spectra = lax.dot_general(dft_ref[...], tail[...], contract, preferred_element_type=F32)
    for r in range(2):
        wide[pl.ds(16 + r, POINTS, stride=ROWS), :] = spectra[r * POINTS : (r + 1) * POINTS]
    chunk = POINTS * ROWS // 8
    writes = []
    for c in range(8):
        here = pl.ds(c * chunk, chunk)
        packed[here] = wide[c * chunk : (c + 1) * chunk, :].astype(BF16)
        writes.append(pltpu.make_async_copy(packed.at[here], out_hbm.at[here], sems.at[4 + c]))
        writes[-1].start()
    for write in writes:
        write.wait()


def filter_bank(voltages, fir_taps):
    rows = POINTS * ROWS
    return pl.pallas_call(
        filter_kernel,
        out_shape=jax.ShapeDtypeStruct((rows, LANES), BF16),
        in_specs=[HBM, HBM, HBM],
        out_specs=HBM,
        scratch_shapes=[
            pltpu.VMEM(voltages.shape, BF16),
            pltpu.VMEM(fir_taps.shape, F32),
            pltpu.VMEM((2 * POINTS, 2 * POINTS), BF16),
            pltpu.VMEM((2, 2, 2 * EDGE + voltages.shape[1], POINTS), F32),
            pltpu.VMEM((LANES, 2 * POINTS), BF16),
            pltpu.VMEM((rows, LANES), F32),
            pltpu.VMEM((rows, LANES), BF16),
            pltpu.SemaphoreType.DMA((12,)),
        ],
        name="filter_bank",
        **params(2 * 256 * 256 * 1024, 1 << 20, 66_000_000),
    )(voltages, fir_taps, dft_matrix(POINTS))


def steering_kernel(chan_ref, u_ref, v_ref, l_ref, m_ref, *out_refs):
    freq = POINTS + chan_ref[0]
    rows = lax.broadcasted_iota(jnp.int32, (STATIONS, STATIONS), 0)
    cols = lax.broadcasted_iota(jnp.int32, (STATIONS, STATIONS), 1)
    eye = rows == cols

    def column(ref):
        return jnp.sum(jnp.where(eye, ref[...], 0), axis=1, keepdims=True)

    def phases(station, pixel):
        index = (freq * ((station * pixel) & (GRID - 1))) & (GRID - 1)
        angle = index.astype(F32) * (2.0 * math.pi / GRID)
        return jnp.cos(angle), jnp.sin(angle)

    l_cos, l_sin = phases(column(u_ref), l_ref[...])
    m_cos, m_sin = phases(column(v_ref), m_ref[...])
    first = lax.broadcasted_iota(jnp.int32, (STATIONS, LANES), 1) < 64
    blocks = out_refs[0].shape[1] // LANES
    for q in range(2 * blocks):
        cos_ref, sin_ref = out_refs[2 * (q // blocks) : 2 * (q // blocks) + 2]
        at = q % blocks * LANES
        a_cos = jnp.where(first, l_cos[:, 2 * q : 2 * q + 1], l_cos[:, 2 * q + 1 : 2 * q + 2])
        a_sin = jnp.where(first, l_sin[:, 2 * q : 2 * q + 1], l_sin[:, 2 * q + 1 : 2 * q + 2])
        cos_ref[:, at : at + LANES] = (a_cos * m_cos - a_sin * m_sin).astype(BF16)
        sin_ref[:, at : at + LANES] = (a_sin * m_cos + a_cos * m_sin).astype(BF16)


def steering(channel, station_u, station_v, rows_l, pixel_m, pixels):
    out = jax.ShapeDtypeStruct((STATIONS, pixels), BF16)
    return pl.pallas_call(
        steering_kernel,
        out_shape=(out,) * 4,
        in_specs=[SMEM] + [VMEM] * 4,
        out_specs=(VMEM,) * 4,
        name="steering",
        **params(12 * STATIONS * pixels, 8 * STATIONS * pixels),
    )(channel, station_u, station_v, rows_l, pixel_m)


def gram_kernel(recv_ref, station_ref, after_ref, out_ref, wide, slots):
    chunk = 256
    for c in range(0, POINTS * ROWS, chunk):
        wide[c : c + chunk, :] = recv_ref[c : c + chunk].astype(F32)
    lane = lax.broadcasted_iota(jnp.int32, (POINTS, LANES), 1)
    head = lane < TAPS - 1
    edge = lane < EDGE
    left_out = jnp.logical_and(head, lax.axis_index("pix") > 0)

    def column(row):
        return wide[pl.ds(row, POINTS, stride=ROWS), :]

    for s in range(2):
        rows = slice(s * POINTS, (s + 1) * POINTS)
        for q in range(8):
            values = column(s * 8 + q)
            if q % 4 == 0:
                values = jnp.where(left_out, 0.0, values)
            slots[rows, q * LANES : (q + 1) * LANES] = values.astype(BF16)
        pieces = [
            pltpu.roll(column(16 + r), LANES - EDGE, 1) if s else column(16 + r) for r in range(2)
        ]
        pieces = [jnp.where(edge, piece, 0.0) for piece in pieces]
        pieces += [jnp.where(head, column(s * 8 + r * 4), 0.0) for r in range(2)]
        total = pieces[0]
        for i in range(1, 4):
            total = total + pltpu.roll(pieces[i], i * EDGE, 1)
        slots[rows, 8 * LANES :] = total.astype(BF16)
    rows = lax.broadcasted_iota(jnp.int32, (STATIONS, STATIONS), 0)
    select = jnp.where(rows == station_ref[...], 1.0, 0.0).astype(BF16)
    ordered = jnp.dot(select, slots[...], preferred_element_type=F32).astype(BF16)
    half = 4 * LANES
    spectra = ordered[:, : 2 * half]
    turned = jnp.concatenate([ordered[:, half : 2 * half], -ordered[:, :half]], axis=1)
    contract = (((1,), (1,)), ((), ()))
    real = lax.dot_general(spectra, spectra, contract, preferred_element_type=F32)
    imag = lax.dot_general(turned, spectra, contract, preferred_element_type=F32)
    out_ref[:, 0:STATIONS] = real.astype(BF16)
    out_ref[:, STATIONS : 2 * STATIONS] = imag.astype(BF16)
    out_ref[:, 2 * STATIONS :] = ordered[:, 2 * half :]


def gram(received, station_row, after):
    return pl.pallas_call(
        gram_kernel,
        out_shape=jax.ShapeDtypeStruct((STATIONS, 2 * STATIONS + LANES), BF16),
        in_specs=[VMEM, VMEM, ANY],
        out_specs=VMEM,
        scratch_shapes=[
            pltpu.VMEM((POINTS * ROWS, LANES), F32),
            pltpu.VMEM((STATIONS, 9 * LANES), BF16),
        ],
        name="gram",
        **params(6 * 256 * 256 * 1024, 1 << 20),
    )(received, station_row, after)


def chip_sums(own_ref, other_ref, real, imag):
    pix = lax.axis_index("pix")
    lane = lax.broadcasted_iota(jnp.int32, (STATIONS, LANES), 1)
    contract = (((1,), (1,)), ((), ()))
    upper_core = (pix & 1) == 1
    own_edge = own_ref[:, 2 * STATIONS :].astype(F32)
    other_edge = other_ref[:, 2 * STATIONS :].astype(F32)
    low = jnp.where(upper_core, other_edge, own_edge)
    high = jnp.where(upper_core, own_edge, other_edge)
    outer = jnp.where(pix >= 2, pltpu.roll(low, LANES - 16, 1), high)
    outer = jnp.where(lane < 16, outer, 0.0).T[0:16]
    inner = jnp.where(lane < 16, low + pltpu.roll(high, LANES - 16, 1), 0.0)
    turned = jnp.where(lane < 8, pltpu.roll(inner, LANES - 8, 1), -pltpu.roll(inner, 8, 1))
    turned = jnp.where(lane < 16, turned, 0.0).astype(BF16)
    inner = inner.astype(BF16)
    real[...] = (
        own_ref[:, 0:STATIONS].astype(F32)
        + other_ref[:, 0:STATIONS].astype(F32)
        + lax.dot_general(inner, inner, contract, preferred_element_type=F32)
    )
    imag[...] = (
        own_ref[:, STATIONS : 2 * STATIONS].astype(F32)
        + other_ref[:, STATIONS : 2 * STATIONS].astype(F32)
        + lax.dot_general(turned, inner, contract, preferred_element_type=F32)
    )
    return outer


def partial_image(real, imag, outer, cos_ref, sin_ref, store):
    rows = lax.broadcasted_iota(jnp.int32, (STATIONS, STATIONS), 0)
    cols = lax.broadcasted_iota(jnp.int32, (STATIONS, STATIONS), 1)
    flag_real = jnp.where(rows == cols, 0.0, real[...]).astype(BF16)
    flag_real = jnp.concatenate([flag_real, outer.astype(BF16)], axis=0)
    flag_imag = jnp.where(rows == cols, 0.0, imag[...]).astype(BF16)
    width = STATIONS
    for q in range(cos_ref.shape[1] // width):
        cosine = cos_ref[:, q * width : (q + 1) * width]
        sine = sin_ref[:, q * width : (q + 1) * width]
        by_cos = jnp.dot(flag_real, cosine, preferred_element_type=F32)
        by_sin = jnp.dot(flag_real, sine, preferred_element_type=F32)
        cross = jnp.dot(flag_imag, sine, preferred_element_type=F32)
        upper = by_cos[:STATIONS] + 2.0 * cross
        pixel = jnp.sum(
            cosine.astype(F32) * upper + sine.astype(F32) * by_sin[:STATIONS], axis=0, keepdims=True
        )
        first = by_cos[STATIONS : STATIONS + 8] - by_sin[STATIONS + 8 :]
        second = by_cos[STATIONS + 8 :] + by_sin[STATIONS : STATIONS + 8]
        store(q, first + pltpu.roll(second, 4, 0), pixel)


def send_kernel(own_ref, other_ref, cos_ref, sin_ref, send_ref, real, imag):
    groups = cos_ref.shape[1] // STATIONS
    count = STATIONS // 4
    outer = chip_sums(own_ref, other_ref, real, imag)
    across = pl.ds(pl.multiple_of((lax.axis_index("pix") ^ 2) * count, count), count)
    send_ref[0:count, :] = real[across, :].astype(BF16)
    send_ref[count : 2 * count, :] = imag[across, :].astype(BF16)
    base = 2 * count
    edge = base + 8 * groups
    send_ref[edge : edge + 8, :] = (outer[0:8] + pltpu.roll(outer[8:16], 4, 0)).astype(BF16)
    send_ref[edge + 8 :, :] = jnp.zeros((send_ref.shape[0] - edge - 8, STATIONS), BF16)

    def store(q, beams, pixel):
        send_ref[base + 8 * q : base + 8 * q + 8, :] = beams.astype(BF16)
        send_ref[edge + 8 + q : edge + 9 + q, :] = pixel.astype(BF16)

    partial_image(real, imag, outer, cos_ref, sin_ref, store)


def keep_kernel(own_ref, other_ref, cos_ref, sin_ref, after_ref, rows_ref, extra_ref, real, imag):
    groups = cos_ref.shape[1] // STATIONS
    count = rows_ref.shape[1]
    outer = chip_sums(own_ref, other_ref, real, imag)
    here = pl.ds(pl.multiple_of(lax.axis_index("pix") * count, count), count)
    rows_ref[0] = real[here, :]
    rows_ref[1] = imag[here, :]
    edge = 8 * groups
    extra_ref[edge : edge + 8, :] = outer[0:8] + pltpu.roll(outer[8:16], 4, 0)

    def store(q, beams, pixel):
        extra_ref[8 * q : 8 * q + 8, :] = beams
        extra_ref[edge + 8 + q : edge + 9 + q, :] = pixel

    partial_image(real, imag, outer, cos_ref, sin_ref, store)


def send_part(own, other, cosine, sine, count):
    groups = cosine.shape[1] // STATIONS
    return pl.pallas_call(
        send_kernel,
        out_shape=jax.ShapeDtypeStruct((2 * count + 8 * groups + 16, STATIONS), BF16),
        in_specs=[VMEM] * 4,
        out_specs=VMEM,
        scratch_shapes=[pltpu.VMEM((STATIONS, STATIONS), F32)] * 2,
        name="send_part",
        **params(6 * 256 * 256 * 1024, 1 << 20),
    )(own, other, cosine, sine)


def keep_part(own, other, cosine, sine, after, count):
    groups = cosine.shape[1] // STATIONS
    return pl.pallas_call(
        keep_kernel,
        out_shape=(
            jax.ShapeDtypeStruct((2, count, STATIONS), F32),
            jax.ShapeDtypeStruct((9 * groups + 8, STATIONS), F32),
        ),
        in_specs=[VMEM] * 4 + [ANY],
        out_specs=(VMEM, VMEM),
        scratch_shapes=[pltpu.VMEM((STATIONS, STATIONS), F32)] * 2,
        name="keep_part",
        **params(6 * 256 * 256 * 1024, 1 << 20),
    )(own, other, cosine, sine, after)


def finish_kernel(inv_total, image_scale, rows_ref, extra_ref, got_ref, vis_ref, image_ref, turn):
    pix = lax.axis_index("pix")
    count = rows_ref.shape[1]
    groups = image_ref.shape[1] // STATIONS
    at = 8 * groups
    edge = extra_ref[at : at + 8, :] + got_ref[2 * count + at : 2 * count + at + 8, :].astype(F32)
    swapped = pltpu.roll(edge, 4, 0)
    low = lax.broadcasted_iota(jnp.int32, (8, STATIONS), 0) < 4
    turn[...] = jnp.concatenate([edge, jnp.where(low, swapped, -swapped)], axis=0).T
    left = turn[pl.ds(pl.multiple_of(pix * count, count), count), :]
    right = jnp.concatenate([edge, edge], axis=0).astype(BF16)
    lane = lax.broadcasted_iota(jnp.int32, left.shape, 1)
    for part in range(2):
        got = got_ref[part * count : (part + 1) * count, :].astype(F32)
        chosen = jnp.where((lane < 8) if part == 0 else (lane >= 8), left, 0.0).astype(BF16)
        update = jnp.dot(chosen, right, preferred_element_type=F32)
        vis_ref[0, part] = (rows_ref[part] + got + update) * inv_total
    own_power = jnp.sum(jnp.sum(edge * edge, axis=1, keepdims=True), axis=0, keepdims=True)
    for q in range(groups):
        got = got_ref[2 * count + at + 8 + q : 2 * count + at + 9 + q, :].astype(F32)
        beams = extra_ref[8 * q : 8 * q + 8, :] + got_ref[
            2 * count + 8 * q : 2 * count + 8 * q + 8, :
        ].astype(F32)
        power = jnp.sum(beams * beams, axis=0, keepdims=True) - own_power
        image_ref[:, q * STATIONS : (q + 1) * STATIONS] = (
            extra_ref[at + 8 + q : at + 9 + q, :] + got + power
        ) * (inv_total * image_scale)


def finish(rows, extra, got, pixels, inv_total, image_scale):
    count = rows.shape[1]
    return pl.pallas_call(
        lambda *refs: finish_kernel(inv_total, image_scale, *refs),
        out_shape=(
            jax.ShapeDtypeStruct((1, 2, count, STATIONS), F32),
            jax.ShapeDtypeStruct((1, pixels), F32),
        ),
        in_specs=[VMEM] * 3,
        out_specs=(VMEM, VMEM),
        scratch_shapes=[pltpu.VMEM((STATIONS, 16), F32)],
        name="finish",
        **params(1 << 20, 1 << 18),
    )(rows, extra, got)


def on_device(voltages, fir_taps, station_of_slot, station_u, station_v, pixel_l, pixel_m):
    spec_dev = voltages.shape[1]
    pix_count = lax.axis_size("pix")
    spectra_total = spec_dev * pix_count
    pix = lax.axis_index("pix")
    across = jnp.where(pix < 2, pix + 2, pix - 2)
    rows_l = pixel_l.shape[0] // pix_count
    sent = filter_bank(voltages, fir_taps).reshape(POINTS, ROWS // 2, 2, LANES)
    received = lax.all_to_all(
        sent, "chan", split_axis=0, concat_axis=0, tiled=True, axis_index_groups=[BACKWARDS]
    )

    block_l = jnp.concatenate(
        [
            lax.dynamic_slice_in_dim(pixel_l, pix * rows_l, rows_l, 0),
            lax.dynamic_slice_in_dim(pixel_l, across * rows_l, rows_l, 0),
            jnp.zeros((LANES - 2 * rows_l,), jnp.int32),
        ]
    )[None]
    pixels = rows_l * pixel_m.shape[0]
    here_cos, here_sin, across_cos, across_sin = steering(
        lax.axis_index("chan")[None].astype(jnp.int32),
        station_u[None],
        station_v[None],
        block_l,
        jnp.concatenate([pixel_m, pixel_m])[None],
        pixels,
    )
    station_row = station_of_slot.reshape(POINTS, 2)[::-1].T.reshape(1, STATIONS)
    own = gram(received.reshape(-1, LANES), station_row, here_cos)
    other = lax.ppermute(own, "pix", [(0, 1), (1, 0), (2, 3), (3, 2)])
    count = STATIONS // pix_count
    send = send_part(own, other, across_cos, across_sin, count)
    got = lax.ppermute(send, "pix", [(0, 2), (2, 0), (1, 3), (3, 1)])
    rows, extra = keep_part(own, other, here_cos, here_sin, send, count)
    return finish(rows, extra, got, pixels, 1.0 / spectra_total, math.sqrt(spectra_total) / STATIONS)


def solution(mesh):
    in_specs = (P("chan", "pix", None), P(), P(), P(), P(), P(), P())
    out_specs = (P("chan", None, "pix", None), P("chan", "pix"))
    return jax.shard_map(
        on_device, mesh=mesh, in_specs=in_specs, out_specs=out_specs, check_vma=False
    )
```

```python
import math

import jax
import jax.numpy as jnp
import numpy as np
from jax import lax
from jax.experimental import pallas as pl
from jax.experimental.pallas import tpu as pltpu
from jax.sharding import PartitionSpec as P

POINTS = 128
TAPS = 4
GRID = 1024
LANES = 128
STATIONS = 256
BACKWARDS = list(range(POINTS))[::-1]
EDGE = 8
ROWS = 18

VMEM = pl.BlockSpec(memory_space=pltpu.VMEM)
HBM = pl.BlockSpec(memory_space=pltpu.HBM)
ANY = pl.BlockSpec(memory_space=pl.ANY)
SMEM = pl.BlockSpec(memory_space=pltpu.SMEM)
F32 = jnp.float32
BF16 = jnp.bfloat16


def dft_matrix(points):
    counter = np.arange(points)
    angle = np.mod(counter[:, None] * counter[None, :], points) * (2.0 * math.pi / points)
    cosine, sine = np.cos(angle), np.sin(angle)
    table = np.block([[cosine, sine], [-sine, cosine]]) * points ** (-0.5)
    table = table.reshape(2, points, 2 * points)[:, ::-1].reshape(2 * points, 2 * points)
    return jnp.asarray(table, dtype=F32).astype(BF16)


def params(flops, moved, limit=40 * 1024 * 1024):
    return dict(
        compiler_params=pltpu.CompilerParams(vmem_limit_bytes=limit),
        cost_estimate=pl.CostEstimate(flops=flops, bytes_accessed=moved, transcendentals=0),
    )


def filter_kernel(v_hbm, taps_hbm, dft_hbm, out_hbm, v_ref, taps_ref, dft_ref, ext, tail, wide, packed, sems):
    spec_dev = v_hbm.shape[1]
    step = 256
    pieces = [(s, t) for s in range(2) for t in range(0, spec_dev, step)]
    copies = [pltpu.make_async_copy(v_hbm.at[s], v_ref.at[s], sems.at[s]) for s in range(2)]
    copies.append(pltpu.make_async_copy(taps_hbm, taps_ref, sems.at[2]))
    copies.append(pltpu.make_async_copy(dft_hbm, dft_ref, sems.at[3]))
    for i in (2, 0, 3, 1):
        copies[i].start()
    contract = (((1,), (1,)), ((), ()))
    blank = jnp.zeros((EDGE, POINTS), F32)
    for s in range(2):
        for half in range(2):
            ext[s, half, 0:EDGE, :] = blank
            ext[s, half, EDGE + spec_dev :, :] = blank
    tail[2 * EDGE :, :] = jnp.zeros((LANES - 2 * EDGE, 2 * POINTS), BF16)
    copies[2].wait()
    taps = taps_ref[...]

    def filtered(s, start, count):
        halves = []
        for half in range(2):
            total = taps[0:1] * ext[s, half, EDGE + start : EDGE + start + count, :]
            for k in range(1, TAPS):
                first = EDGE - k + start
                total = total + taps[k : k + 1] * ext[s, half, first : first + count, :]
            halves.append(total.astype(BF16))
        return jnp.concatenate(halves, axis=1)

    for i, (s, t) in enumerate(pieces):
        if t == 0:
            copies[s].wait()
            for half in range(2):
                ext[s, half, EDGE : EDGE + spec_dev, :] = v_ref[
                    s, :, half * POINTS : (half + 1) * POINTS
                ].astype(F32)
        if i == 0:
            copies[3].wait()
        spectra = lax.dot_general(
            dft_ref[...], filtered(s, t, step), contract, preferred_element_type=F32
        )
        for r in range(2):
            for part in range(step // LANES):
                row = s * 8 + r * 4 + t // LANES + part
                wide[pl.ds(row, POINTS, stride=ROWS), :] = spectra[
                    r * POINTS : (r + 1) * POINTS, part * LANES : (part + 1) * LANES
                ]
    tail[0 : 2 * EDGE, :] = jnp.concatenate([filtered(s, spec_dev, EDGE) for s in range(2)], axis=0)
    spectra = lax.dot_general(dft_ref[...], tail[...], contract, preferred_element_type=F32)
    for r in range(2):
        wide[pl.ds(16 + r, POINTS, stride=ROWS), :] = spectra[r * POINTS : (r + 1) * POINTS]
    chunk = POINTS * ROWS // 8
    writes = []
    for c in range(8):
        here = pl.ds(c * chunk, chunk)
        packed[here] = wide[c * chunk : (c + 1) * chunk, :].astype(BF16)
        writes.append(pltpu.make_async_copy(packed.at[here], out_hbm.at[here], sems.at[4 + c]))
        writes[-1].start()
    for write in writes:
        write.wait()


def filter_bank(voltages, fir_taps):
    rows = POINTS * ROWS
    return pl.pallas_call(
        filter_kernel,
        out_shape=jax.ShapeDtypeStruct((rows, LANES), BF16),
        in_specs=[HBM, HBM, HBM],
        out_specs=HBM,
        scratch_shapes=[
            pltpu.VMEM(voltages.shape, BF16),
            pltpu.VMEM(fir_taps.shape, F32),
            pltpu.VMEM((2 * POINTS, 2 * POINTS), BF16),
            pltpu.VMEM((2, 2, 2 * EDGE + voltages.shape[1], POINTS), F32),
            pltpu.VMEM((LANES, 2 * POINTS), BF16),
            pltpu.VMEM((rows, LANES), F32),
            pltpu.VMEM((rows, LANES), BF16),
            pltpu.SemaphoreType.DMA((12,)),
        ],
        name="filter_bank",
        **params(2 * 256 * 256 * 1024, 1 << 20, 66_000_000),
    )(voltages, fir_taps, dft_matrix(POINTS))


def steering_kernel(chan_ref, u_ref, v_ref, l_ref, m_ref, *out_refs):
    freq = POINTS + chan_ref[0]
    rows = lax.broadcasted_iota(jnp.int32, (STATIONS, STATIONS), 0)
    cols = lax.broadcasted_iota(jnp.int32, (STATIONS, STATIONS), 1)
    eye = rows == cols

    def column(ref):
        return jnp.sum(jnp.where(eye, ref[...], 0), axis=1, keepdims=True)

    def phases(station, pixel):
        index = (freq * ((station * pixel) & (GRID - 1))) & (GRID - 1)
        angle = index.astype(F32) * (2.0 * math.pi / GRID)
        return jnp.cos(angle), jnp.sin(angle)

    l_cos, l_sin = phases(column(u_ref), l_ref[...])
    m_cos, m_sin = phases(column(v_ref), m_ref[...])
    first = lax.broadcasted_iota(jnp.int32, (STATIONS, LANES), 1) < 64
    blocks = out_refs[0].shape[1] // LANES
    for q in range(2 * blocks):
        cos_ref, sin_ref = out_refs[2 * (q // blocks) : 2 * (q // blocks) + 2]
        at = q % blocks * LANES
        a_cos = jnp.where(first, l_cos[:, 2 * q : 2 * q + 1], l_cos[:, 2 * q + 1 : 2 * q + 2])
        a_sin = jnp.where(first, l_sin[:, 2 * q : 2 * q + 1], l_sin[:, 2 * q + 1 : 2 * q + 2])
        cos_ref[:, at : at + LANES] = (a_cos * m_cos - a_sin * m_sin).astype(BF16)
        sin_ref[:, at : at + LANES] = (a_sin * m_cos + a_cos * m_sin).astype(BF16)


def steering(channel, station_u, station_v, rows_l, pixel_m, pixels):
    out = jax.ShapeDtypeStruct((STATIONS, pixels), BF16)
    return pl.pallas_call(
        steering_kernel,
        out_shape=(out,) * 4,
        in_specs=[SMEM] + [VMEM] * 4,
        out_specs=(VMEM,) * 4,
        name="steering",
        **params(12 * STATIONS * pixels, 8 * STATIONS * pixels),
    )(channel, station_u, station_v, rows_l, pixel_m)


def gram_kernel(recv_ref, station_ref, after_ref, out_ref, wide, slots):
    chunk = 256
    for c in range(0, POINTS * ROWS, chunk):
        wide[c : c + chunk, :] = recv_ref[c : c + chunk].astype(F32)
    lane = lax.broadcasted_iota(jnp.int32, (POINTS, LANES), 1)
    head = lane < TAPS - 1
    edge = lane < EDGE
    left_out = jnp.logical_and(head, lax.axis_index("pix") > 0)

    def column(row):
        return wide[pl.ds(row, POINTS, stride=ROWS), :]

    for s in range(2):
        rows = slice(s * POINTS, (s + 1) * POINTS)
        for q in range(8):
            values = column(s * 8 + q)
            if q % 4 == 0:
                values = jnp.where(left_out, 0.0, values)
            slots[rows, q * LANES : (q + 1) * LANES] = values.astype(BF16)
        pieces = [
            pltpu.roll(column(16 + r), LANES - EDGE, 1) if s else column(16 + r) for r in range(2)
        ]
        pieces = [jnp.where(edge, piece, 0.0) for piece in pieces]
        pieces += [jnp.where(head, column(s * 8 + r * 4), 0.0) for r in range(2)]
        total = pieces[0]
        for i in range(1, 4):
            total = total + pltpu.roll(pieces[i], i * EDGE, 1)
        slots[rows, 8 * LANES :] = total.astype(BF16)
    rows = lax.broadcasted_iota(jnp.int32, (STATIONS, STATIONS), 0)
    select = jnp.where(rows == station_ref[...], 1.0, 0.0).astype(BF16)
    ordered = jnp.dot(select, slots[...], preferred_element_type=F32).astype(BF16)
    half = 4 * LANES
    spectra = ordered[:, : 2 * half]
    contract = (((1,), (1,)), ((), ()))
    cross = lax.dot_general(
        ordered[:, half : 2 * half], ordered[:, :half], contract, preferred_element_type=F32
    )
    real = lax.dot_general(spectra, spectra, contract, preferred_element_type=F32)
    imag = cross - cross.T
    out_ref[:, 0:STATIONS] = real.astype(BF16)
    out_ref[:, STATIONS : 2 * STATIONS] = imag.astype(BF16)
    out_ref[:, 2 * STATIONS :] = ordered[:, 2 * half :]


def gram(received, station_row, after):
    return pl.pallas_call(
        gram_kernel,
        out_shape=jax.ShapeDtypeStruct((STATIONS, 2 * STATIONS + LANES), BF16),
        in_specs=[VMEM, VMEM, ANY],
        out_specs=VMEM,
        scratch_shapes=[
            pltpu.VMEM((POINTS * ROWS, LANES), F32),
            pltpu.VMEM((STATIONS, 9 * LANES), BF16),
        ],
        name="gram",
        **params(6 * 256 * 256 * 1024, 1 << 20),
    )(received, station_row, after)


def chip_sums(own_ref, other_ref, real, imag):
    pix = lax.axis_index("pix")
    lane = lax.broadcasted_iota(jnp.int32, (STATIONS, LANES), 1)
    contract = (((1,), (1,)), ((), ()))
    upper_core = (pix & 1) == 1
    own_edge = own_ref[:, 2 * STATIONS :].astype(F32)
    other_edge = other_ref[:, 2 * STATIONS :].astype(F32)
    low = jnp.where(upper_core, other_edge, own_edge)
    high = jnp.where(upper_core, own_edge, other_edge)
    outer = jnp.where(pix >= 2, pltpu.roll(low, LANES - 16, 1), high)
    outer = jnp.where(lane < 16, outer, 0.0).T[0:16]
    inner = jnp.where(lane < 16, low + pltpu.roll(high, LANES - 16, 1), 0.0)
    turned = jnp.where(lane < 8, pltpu.roll(inner, LANES - 8, 1), -pltpu.roll(inner, 8, 1))
    turned = jnp.where(lane < 16, turned, 0.0).astype(BF16)
    inner = inner.astype(BF16)
    real[...] = (
        own_ref[:, 0:STATIONS].astype(F32)
        + other_ref[:, 0:STATIONS].astype(F32)
        + lax.dot_general(inner, inner, contract, preferred_element_type=F32)
    )
    imag[...] = (
        own_ref[:, STATIONS : 2 * STATIONS].astype(F32)
        + other_ref[:, STATIONS : 2 * STATIONS].astype(F32)
        + lax.dot_general(turned, inner, contract, preferred_element_type=F32)
    )
    return outer


def partial_image(real, imag, outer, cos_ref, sin_ref, store):
    rows = lax.broadcasted_iota(jnp.int32, (STATIONS, STATIONS), 0)
    cols = lax.broadcasted_iota(jnp.int32, (STATIONS, STATIONS), 1)
    flag_real = jnp.where(rows == cols, 0.0, real[...]).astype(BF16)
    flag_real = jnp.concatenate([flag_real, outer.astype(BF16)], axis=0)
    flag_imag = jnp.where(rows == cols, 0.0, imag[...]).astype(BF16)
    width = STATIONS
    for q in range(cos_ref.shape[1] // width):
        cosine = cos_ref[:, q * width : (q + 1) * width]
        sine = sin_ref[:, q * width : (q + 1) * width]
        by_cos = jnp.dot(flag_real, cosine, preferred_element_type=F32)
        by_sin = jnp.dot(flag_real, sine, preferred_element_type=F32)
        cross = jnp.dot(flag_imag, sine, preferred_element_type=F32)
        upper = by_cos[:STATIONS] + 2.0 * cross
        pixel = jnp.sum(
            cosine.astype(F32) * upper + sine.astype(F32) * by_sin[:STATIONS], axis=0, keepdims=True
        )
        first = by_cos[STATIONS : STATIONS + 8] - by_sin[STATIONS + 8 :]
        second = by_cos[STATIONS + 8 :] + by_sin[STATIONS : STATIONS + 8]
        store(q, first + pltpu.roll(second, 4, 0), pixel)


def send_kernel(own_ref, other_ref, cos_ref, sin_ref, send_ref, real, imag):
    groups = cos_ref.shape[1] // STATIONS
    count = STATIONS // 4
    outer = chip_sums(own_ref, other_ref, real, imag)
    across = pl.ds(pl.multiple_of((lax.axis_index("pix") ^ 2) * count, count), count)
    send_ref[0:count, :] = real[across, :].astype(BF16)
    send_ref[count : 2 * count, :] = imag[across, :].astype(BF16)
    base = 2 * count
    edge = base + 8 * groups
    send_ref[edge : edge + 8, :] = (outer[0:8] + pltpu.roll(outer[8:16], 4, 0)).astype(BF16)
    send_ref[edge + 8 :, :] = jnp.zeros((send_ref.shape[0] - edge - 8, STATIONS), BF16)

    def store(q, beams, pixel):
        send_ref[base + 8 * q : base + 8 * q + 8, :] = beams.astype(BF16)
        send_ref[edge + 8 + q : edge + 9 + q, :] = pixel.astype(BF16)

    partial_image(real, imag, outer, cos_ref, sin_ref, store)


def keep_kernel(own_ref, other_ref, cos_ref, sin_ref, after_ref, rows_ref, extra_ref, real, imag):
    groups = cos_ref.shape[1] // STATIONS
    count = rows_ref.shape[1]
    outer = chip_sums(own_ref, other_ref, real, imag)
    here = pl.ds(pl.multiple_of(lax.axis_index("pix") * count, count), count)
    rows_ref[0] = real[here, :]
    rows_ref[1] = imag[here, :]
    edge = 8 * groups
    extra_ref[edge : edge + 8, :] = outer[0:8] + pltpu.roll(outer[8:16], 4, 0)

    def store(q, beams, pixel):
        extra_ref[8 * q : 8 * q + 8, :] = beams
        extra_ref[edge + 8 + q : edge + 9 + q, :] = pixel

    partial_image(real, imag, outer, cos_ref, sin_ref, store)


def send_part(own, other, cosine, sine, count):
    groups = cosine.shape[1] // STATIONS
    return pl.pallas_call(
        send_kernel,
        out_shape=jax.ShapeDtypeStruct((2 * count + 8 * groups + 16, STATIONS), BF16),
        in_specs=[VMEM] * 4,
        out_specs=VMEM,
        scratch_shapes=[pltpu.VMEM((STATIONS, STATIONS), F32)] * 2,
        name="send_part",
        **params(6 * 256 * 256 * 1024, 1 << 20),
    )(own, other, cosine, sine)


def keep_part(own, other, cosine, sine, after, count):
    groups = cosine.shape[1] // STATIONS
    return pl.pallas_call(
        keep_kernel,
        out_shape=(
            jax.ShapeDtypeStruct((2, count, STATIONS), F32),
            jax.ShapeDtypeStruct((9 * groups + 8, STATIONS), F32),
        ),
        in_specs=[VMEM] * 4 + [ANY],
        out_specs=(VMEM, VMEM),
        scratch_shapes=[pltpu.VMEM((STATIONS, STATIONS), F32)] * 2,
        name="keep_part",
        **params(6 * 256 * 256 * 1024, 1 << 20),
    )(own, other, cosine, sine, after)


def finish_kernel(inv_total, image_scale, rows_ref, extra_ref, got_ref, vis_ref, image_ref, turn):
    pix = lax.axis_index("pix")
    count = rows_ref.shape[1]
    groups = image_ref.shape[1] // STATIONS
    at = 8 * groups
    edge = extra_ref[at : at + 8, :] + got_ref[2 * count + at : 2 * count + at + 8, :].astype(F32)
    swapped = pltpu.roll(edge, 4, 0)
    low = lax.broadcasted_iota(jnp.int32, (8, STATIONS), 0) < 4
    turn[...] = jnp.concatenate([edge, jnp.where(low, swapped, -swapped)], axis=0).T
    left = turn[pl.ds(pl.multiple_of(pix * count, count), count), :]
    right = jnp.concatenate([edge, edge], axis=0).astype(BF16)
    lane = lax.broadcasted_iota(jnp.int32, left.shape, 1)
    for part in range(2):
        got = got_ref[part * count : (part + 1) * count, :].astype(F32)
        chosen = jnp.where((lane < 8) if part == 0 else (lane >= 8), left, 0.0).astype(BF16)
        update = jnp.dot(chosen, right, preferred_element_type=F32)
        vis_ref[0, part] = (rows_ref[part] + got + update) * inv_total
    own_power = jnp.sum(jnp.sum(edge * edge, axis=1, keepdims=True), axis=0, keepdims=True)
    for q in range(groups):
        got = got_ref[2 * count + at + 8 + q : 2 * count + at + 9 + q, :].astype(F32)
        beams = extra_ref[8 * q : 8 * q + 8, :] + got_ref[
            2 * count + 8 * q : 2 * count + 8 * q + 8, :
        ].astype(F32)
        power = jnp.sum(beams * beams, axis=0, keepdims=True) - own_power
        image_ref[:, q * STATIONS : (q + 1) * STATIONS] = (
            extra_ref[at + 8 + q : at + 9 + q, :] + got + power
        ) * (inv_total * image_scale)


def finish(rows, extra, got, pixels, inv_total, image_scale):
    count = rows.shape[1]
    return pl.pallas_call(
        lambda *refs: finish_kernel(inv_total, image_scale, *refs),
        out_shape=(
            jax.ShapeDtypeStruct((1, 2, count, STATIONS), F32),
            jax.ShapeDtypeStruct((1, pixels), F32),
        ),
        in_specs=[VMEM] * 3,
        out_specs=(VMEM, VMEM),
        scratch_shapes=[pltpu.VMEM((STATIONS, 16), F32)],
        name="finish",
        **params(1 << 20, 1 << 18),
    )(rows, extra, got)


def on_device(voltages, fir_taps, station_of_slot, station_u, station_v, pixel_l, pixel_m):
    spec_dev = voltages.shape[1]
    pix_count = lax.axis_size("pix")
    spectra_total = spec_dev * pix_count
    pix = lax.axis_index("pix")
    across = jnp.where(pix < 2, pix + 2, pix - 2)
    rows_l = pixel_l.shape[0] // pix_count
    sent = filter_bank(voltages, fir_taps).reshape(POINTS, ROWS // 2, 2, LANES)
    received = lax.all_to_all(
        sent, "chan", split_axis=0, concat_axis=0, tiled=True, axis_index_groups=[BACKWARDS]
    )

    block_l = jnp.concatenate(
        [
            lax.dynamic_slice_in_dim(pixel_l, pix * rows_l, rows_l, 0),
            lax.dynamic_slice_in_dim(pixel_l, across * rows_l, rows_l, 0),
            jnp.zeros((LANES - 2 * rows_l,), jnp.int32),
        ]
    )[None]
    pixels = rows_l * pixel_m.shape[0]
    here_cos, here_sin, across_cos, across_sin = steering(
        lax.axis_index("chan")[None].astype(jnp.int32),
        station_u[None],
        station_v[None],
        block_l,
        jnp.concatenate([pixel_m, pixel_m])[None],
        pixels,
    )
    station_row = station_of_slot.reshape(POINTS, 2)[::-1].T.reshape(1, STATIONS)
    own = gram(received.reshape(-1, LANES), station_row, here_cos)
    other = lax.ppermute(own, "pix", [(0, 1), (1, 0), (2, 3), (3, 2)])
    count = STATIONS // pix_count
    send = send_part(own, other, across_cos, across_sin, count)
    got = lax.ppermute(send, "pix", [(0, 2), (2, 0), (1, 3), (3, 1)])
    rows, extra = keep_part(own, other, here_cos, here_sin, send, count)
    return finish(rows, extra, got, pixels, 1.0 / spectra_total, math.sqrt(spectra_total) / STATIONS)


def solution(mesh):
    in_specs = (P("chan", "pix", None), P(), P(), P(), P(), P(), P())
    out_specs = (P("chan", None, "pix", None), P("chan", "pix"))
    return jax.shard_map(
        on_device, mesh=mesh, in_specs=in_specs, out_specs=out_specs, check_vma=False
    )
```

```python
import math

import jax
import jax.numpy as jnp
import numpy as np
from jax import lax
from jax.experimental import pallas as pl
from jax.experimental.pallas import tpu as pltpu
from jax.sharding import PartitionSpec as P

POINTS = 128
TAPS = 4
GRID = 1024
LANES = 128
STATIONS = 256
BACKWARDS = list(range(POINTS))[::-1]
EDGE = 8
ROWS = 18

VMEM = pl.BlockSpec(memory_space=pltpu.VMEM)
HBM = pl.BlockSpec(memory_space=pltpu.HBM)
ANY = pl.BlockSpec(memory_space=pl.ANY)
SMEM = pl.BlockSpec(memory_space=pltpu.SMEM)
F32 = jnp.float32
BF16 = jnp.bfloat16


def dft_matrix(points):
    counter = np.arange(points)
    angle = np.mod(counter[:, None] * counter[None, :], points) * (2.0 * math.pi / points)
    cosine, sine = np.cos(angle), np.sin(angle)
    table = np.block([[cosine, sine], [-sine, cosine]]) * points ** (-0.5)
    table = table.reshape(2, points, 2 * points)[:, ::-1].reshape(2 * points, 2 * points)
    return jnp.asarray(table, dtype=F32).astype(BF16)


def params(flops, moved, limit=40 * 1024 * 1024):
    return dict(
        compiler_params=pltpu.CompilerParams(vmem_limit_bytes=limit),
        cost_estimate=pl.CostEstimate(flops=flops, bytes_accessed=moved, transcendentals=0),
    )


def filter_kernel(v_hbm, taps_hbm, dft_hbm, out_hbm, v_ref, taps_ref, dft_ref, ext, tail, wide, packed, sems):
    spec_dev = v_hbm.shape[1]
    step = 256
    pieces = [(s, t) for s in range(2) for t in range(0, spec_dev, step)]
    copies = [pltpu.make_async_copy(v_hbm.at[s], v_ref.at[s], sems.at[s]) for s in range(2)]
    copies.append(pltpu.make_async_copy(taps_hbm, taps_ref, sems.at[2]))
    copies.append(pltpu.make_async_copy(dft_hbm, dft_ref, sems.at[3]))
    for i in (2, 0, 3, 1):
        copies[i].start()
    contract = (((1,), (1,)), ((), ()))
    blank = jnp.zeros((EDGE, POINTS), F32)
    for s in range(2):
        for half in range(2):
            ext[s, half, 0:EDGE, :] = blank
            ext[s, half, EDGE + spec_dev :, :] = blank
    tail[2 * EDGE :, :] = jnp.zeros((LANES - 2 * EDGE, 2 * POINTS), BF16)
    copies[2].wait()
    taps = taps_ref[...]

    def filtered(s, start, count):
        halves = []
        for half in range(2):
            total = taps[0:1] * ext[s, half, EDGE + start : EDGE + start + count, :]
            for k in range(1, TAPS):
                first = EDGE - k + start
                total = total + taps[k : k + 1] * ext[s, half, first : first + count, :]
            halves.append(total.astype(BF16))
        return jnp.concatenate(halves, axis=1)

    for i, (s, t) in enumerate(pieces):
        if t == 0:
            copies[s].wait()
            for half in range(2):
                ext[s, half, EDGE : EDGE + spec_dev, :] = v_ref[
                    s, :, half * POINTS : (half + 1) * POINTS
                ].astype(F32)
        samples = filtered(s, t, step)
        if i == 0:
            copies[3].wait()
        spectra = lax.dot_general(dft_ref[...], samples, contract, preferred_element_type=F32)
        for r in range(2):
            for part in range(step // LANES):
                row = s * 8 + r * 4 + t // LANES + part
                wide[pl.ds(row, POINTS, stride=ROWS), :] = spectra[
                    r * POINTS : (r + 1) * POINTS, part * LANES : (part + 1) * LANES
                ]
    tail[0 : 2 * EDGE, :] = jnp.concatenate([filtered(s, spec_dev, EDGE) for s in range(2)], axis=0)
    spectra = lax.dot_general(dft_ref[...], tail[...], contract, preferred_element_type=F32)
    for r in range(2):
        wide[pl.ds(16 + r, POINTS, stride=ROWS), :] = spectra[r * POINTS : (r + 1) * POINTS]
    chunk = POINTS * ROWS // 8
    writes = []
    for c in range(8):
        here = pl.ds(c * chunk, chunk)
        packed[here] = wide[c * chunk : (c + 1) * chunk, :].astype(BF16)
        writes.append(pltpu.make_async_copy(packed.at[here], out_hbm.at[here], sems.at[4 + c]))
        writes[-1].start()
    for write in writes:
        write.wait()


def filter_bank(voltages, fir_taps):
    rows = POINTS * ROWS
    return pl.pallas_call(
        filter_kernel,
        out_shape=jax.ShapeDtypeStruct((rows, LANES), BF16),
        in_specs=[HBM, HBM, HBM],
        out_specs=HBM,
        scratch_shapes=[
            pltpu.VMEM(voltages.shape, BF16),
            pltpu.VMEM(fir_taps.shape, F32),
            pltpu.VMEM((2 * POINTS, 2 * POINTS), BF16),
            pltpu.VMEM((2, 2, 2 * EDGE + voltages.shape[1], POINTS), F32),
            pltpu.VMEM((LANES, 2 * POINTS), BF16),
            pltpu.VMEM((rows, LANES), F32),
            pltpu.VMEM((rows, LANES), BF16),
            pltpu.SemaphoreType.DMA((12,)),
        ],
        name="filter_bank",
        **params(2 * 256 * 256 * 1024, 1 << 20, 66_000_000),
    )(voltages, fir_taps, dft_matrix(POINTS))


def steering_kernel(chan_ref, u_ref, v_ref, l_ref, m_ref, *out_refs):
    freq = POINTS + chan_ref[0]
    rows = lax.broadcasted_iota(jnp.int32, (STATIONS, STATIONS), 0)
    cols = lax.broadcasted_iota(jnp.int32, (STATIONS, STATIONS), 1)
    eye = rows == cols

    def column(ref):
        return jnp.sum(jnp.where(eye, ref[...], 0), axis=1, keepdims=True)

    def phases(station, pixel):
        index = (freq * ((station * pixel) & (GRID - 1))) & (GRID - 1)
        angle = index.astype(F32) * (2.0 * math.pi / GRID)
        return jnp.cos(angle), jnp.sin(angle)

    l_cos, l_sin = phases(column(u_ref), l_ref[...])
    m_cos, m_sin = phases(column(v_ref), m_ref[...])
    first = lax.broadcasted_iota(jnp.int32, (STATIONS, LANES), 1) < 64
    blocks = out_refs[0].shape[1] // LANES
    for q in range(2 * blocks):
        cos_ref, sin_ref = out_refs[2 * (q // blocks) : 2 * (q // blocks) + 2]
        at = q % blocks * LANES
        a_cos = jnp.where(first, l_cos[:, 2 * q : 2 * q + 1], l_cos[:, 2 * q + 1 : 2 * q + 2])
        a_sin = jnp.where(first, l_sin[:, 2 * q : 2 * q + 1], l_sin[:, 2 * q + 1 : 2 * q + 2])
        cos_ref[:, at : at + LANES] = (a_cos * m_cos - a_sin * m_sin).astype(BF16)
        sin_ref[:, at : at + LANES] = (a_sin * m_cos + a_cos * m_sin).astype(BF16)


def steering(channel, station_u, station_v, rows_l, pixel_m, pixels):
    out = jax.ShapeDtypeStruct((STATIONS, pixels), BF16)
    return pl.pallas_call(
        steering_kernel,
        out_shape=(out,) * 4,
        in_specs=[SMEM] + [VMEM] * 4,
        out_specs=(VMEM,) * 4,
        name="steering",
        **params(12 * STATIONS * pixels, 8 * STATIONS * pixels),
    )(channel, station_u, station_v, rows_l, pixel_m)


def gram_kernel(recv_ref, station_ref, after_ref, out_ref, wide, slots):
    chunk = 256
    for c in range(0, POINTS * ROWS, chunk):
        wide[c : c + chunk, :] = recv_ref[c : c + chunk].astype(F32)
    lane = lax.broadcasted_iota(jnp.int32, (POINTS, LANES), 1)
    head = lane < TAPS - 1
    edge = lane < EDGE
    left_out = jnp.logical_and(head, lax.axis_index("pix") > 0)

    def column(row):
        return wide[pl.ds(row, POINTS, stride=ROWS), :]

    for s in range(2):
        rows = slice(s * POINTS, (s + 1) * POINTS)
        for q in range(8):
            values = column(s * 8 + q)
            if q % 4 == 0:
                values = jnp.where(left_out, 0.0, values)
            slots[rows, q * LANES : (q + 1) * LANES] = values.astype(BF16)
        pieces = [
            pltpu.roll(column(16 + r), LANES - EDGE, 1) if s else column(16 + r) for r in range(2)
        ]
        pieces = [jnp.where(edge, piece, 0.0) for piece in pieces]
        pieces += [jnp.where(head, column(s * 8 + r * 4), 0.0) for r in range(2)]
        total = pieces[0]
        for i in range(1, 4):
            total = total + pltpu.roll(pieces[i], i * EDGE, 1)
        slots[rows, 8 * LANES :] = total.astype(BF16)
    rows = lax.broadcasted_iota(jnp.int32, (STATIONS, STATIONS), 0)
    select = jnp.where(rows == station_ref[...], 1.0, 0.0).astype(BF16)
    ordered = jnp.dot(select, slots[...], preferred_element_type=F32).astype(BF16)
    half = 4 * LANES
    spectra = ordered[:, : 2 * half]
    contract = (((1,), (1,)), ((), ()))
    cross = lax.dot_general(
        ordered[:, half : 2 * half], ordered[:, :half], contract, preferred_element_type=F32
    )
    real = lax.dot_general(spectra, spectra, contract, preferred_element_type=F32)
    imag = cross - cross.T
    out_ref[:, 0:STATIONS] = real.astype(BF16)
    out_ref[:, STATIONS : 2 * STATIONS] = imag.astype(BF16)
    out_ref[:, 2 * STATIONS :] = ordered[:, 2 * half :]


def gram(received, station_row, after):
    return pl.pallas_call(
        gram_kernel,
        out_shape=jax.ShapeDtypeStruct((STATIONS, 2 * STATIONS + LANES), BF16),
        in_specs=[VMEM, VMEM, ANY],
        out_specs=VMEM,
        scratch_shapes=[
            pltpu.VMEM((POINTS * ROWS, LANES), F32),
            pltpu.VMEM((STATIONS, 9 * LANES), BF16),
        ],
        name="gram",
        **params(6 * 256 * 256 * 1024, 1 << 20),
    )(received, station_row, after)


def chip_sums(own_ref, other_ref, real, imag):
    pix = lax.axis_index("pix")
    lane = lax.broadcasted_iota(jnp.int32, (STATIONS, LANES), 1)
    contract = (((1,), (1,)), ((), ()))
    upper_core = (pix & 1) == 1
    own_edge = own_ref[:, 2 * STATIONS :].astype(F32)
    other_edge = other_ref[:, 2 * STATIONS :].astype(F32)
    low = jnp.where(upper_core, other_edge, own_edge)
    high = jnp.where(upper_core, own_edge, other_edge)
    outer = jnp.where(pix >= 2, pltpu.roll(low, LANES - 16, 1), high)
    outer = jnp.where(lane < 16, outer, 0.0).T[0:16]
    inner = jnp.where(lane < 16, low + pltpu.roll(high, LANES - 16, 1), 0.0)
    turned = jnp.where(lane < 8, pltpu.roll(inner, LANES - 8, 1), -pltpu.roll(inner, 8, 1))
    turned = jnp.where(lane < 16, turned, 0.0).astype(BF16)
    inner = inner.astype(BF16)
    real[...] = (
        own_ref[:, 0:STATIONS].astype(F32)
        + other_ref[:, 0:STATIONS].astype(F32)
        + lax.dot_general(inner, inner, contract, preferred_element_type=F32)
    )
    imag[...] = (
        own_ref[:, STATIONS : 2 * STATIONS].astype(F32)
        + other_ref[:, STATIONS : 2 * STATIONS].astype(F32)
        + lax.dot_general(turned, inner, contract, preferred_element_type=F32)
    )
    return outer


def partial_image(real, imag, outer, cos_ref, sin_ref, store):
    rows = lax.broadcasted_iota(jnp.int32, (STATIONS, STATIONS), 0)
    cols = lax.broadcasted_iota(jnp.int32, (STATIONS, STATIONS), 1)
    flag_real = jnp.where(rows == cols, 0.0, real[...]).astype(BF16)
    flag_real = jnp.concatenate([flag_real, outer.astype(BF16)], axis=0)
    flag_imag = jnp.where(rows == cols, 0.0, imag[...]).astype(BF16)
    width = STATIONS
    for q in range(cos_ref.shape[1] // width):
        cosine = cos_ref[:, q * width : (q + 1) * width]
        sine = sin_ref[:, q * width : (q + 1) * width]
        by_cos = jnp.dot(flag_real, cosine, preferred_element_type=F32)
        by_sin = jnp.dot(flag_real, sine, preferred_element_type=F32)
        cross = jnp.dot(flag_imag, sine, preferred_element_type=F32)
        upper = by_cos[:STATIONS] + 2.0 * cross
        pixel = jnp.sum(
            cosine.astype(F32) * upper + sine.astype(F32) * by_sin[:STATIONS], axis=0, keepdims=True
        )
        first = by_cos[STATIONS : STATIONS + 8] - by_sin[STATIONS + 8 :]
        second = by_cos[STATIONS + 8 :] + by_sin[STATIONS : STATIONS + 8]
        store(q, first + pltpu.roll(second, 4, 0), pixel)


def send_kernel(own_ref, other_ref, cos_ref, sin_ref, send_ref, real, imag):
    groups = cos_ref.shape[1] // STATIONS
    count = STATIONS // 4
    outer = chip_sums(own_ref, other_ref, real, imag)
    across = pl.ds(pl.multiple_of((lax.axis_index("pix") ^ 2) * count, count), count)
    send_ref[0:count, :] = real[across, :].astype(BF16)
    send_ref[count : 2 * count, :] = imag[across, :].astype(BF16)
    base = 2 * count
    edge = base + 8 * groups
    send_ref[edge : edge + 8, :] = (outer[0:8] + pltpu.roll(outer[8:16], 4, 0)).astype(BF16)
    send_ref[edge + 8 :, :] = jnp.zeros((send_ref.shape[0] - edge - 8, STATIONS), BF16)

    def store(q, beams, pixel):
        send_ref[base + 8 * q : base + 8 * q + 8, :] = beams.astype(BF16)
        send_ref[edge + 8 + q : edge + 9 + q, :] = pixel.astype(BF16)

    partial_image(real, imag, outer, cos_ref, sin_ref, store)


def keep_kernel(own_ref, other_ref, cos_ref, sin_ref, after_ref, rows_ref, extra_ref, real, imag):
    groups = cos_ref.shape[1] // STATIONS
    count = rows_ref.shape[1]
    outer = chip_sums(own_ref, other_ref, real, imag)
    here = pl.ds(pl.multiple_of(lax.axis_index("pix") * count, count), count)
    rows_ref[0] = real[here, :]
    rows_ref[1] = imag[here, :]
    edge = 8 * groups
    extra_ref[edge : edge + 8, :] = outer[0:8] + pltpu.roll(outer[8:16], 4, 0)

    def store(q, beams, pixel):
        extra_ref[8 * q : 8 * q + 8, :] = beams
        extra_ref[edge + 8 + q : edge + 9 + q, :] = pixel

    partial_image(real, imag, outer, cos_ref, sin_ref, store)


def send_part(own, other, cosine, sine, count):
    groups = cosine.shape[1] // STATIONS
    return pl.pallas_call(
        send_kernel,
        out_shape=jax.ShapeDtypeStruct((2 * count + 8 * groups + 16, STATIONS), BF16),
        in_specs=[VMEM] * 4,
        out_specs=VMEM,
        scratch_shapes=[pltpu.VMEM((STATIONS, STATIONS), F32)] * 2,
        name="send_part",
        **params(6 * 256 * 256 * 1024, 1 << 20),
    )(own, other, cosine, sine)


def keep_part(own, other, cosine, sine, after, count):
    groups = cosine.shape[1] // STATIONS
    return pl.pallas_call(
        keep_kernel,
        out_shape=(
            jax.ShapeDtypeStruct((2, count, STATIONS), F32),
            jax.ShapeDtypeStruct((9 * groups + 8, STATIONS), F32),
        ),
        in_specs=[VMEM] * 4 + [ANY],
        out_specs=(VMEM, VMEM),
        scratch_shapes=[pltpu.VMEM((STATIONS, STATIONS), F32)] * 2,
        name="keep_part",
        **params(6 * 256 * 256 * 1024, 1 << 20),
    )(own, other, cosine, sine, after)


def finish_kernel(inv_total, image_scale, rows_ref, extra_ref, got_ref, vis_ref, image_ref, turn):
    pix = lax.axis_index("pix")
    count = rows_ref.shape[1]
    groups = image_ref.shape[1] // STATIONS
    at = 8 * groups
    edge = extra_ref[at : at + 8, :] + got_ref[2 * count + at : 2 * count + at + 8, :].astype(F32)
    swapped = pltpu.roll(edge, 4, 0)
    low = lax.broadcasted_iota(jnp.int32, (8, STATIONS), 0) < 4
    turn[...] = jnp.concatenate([edge, jnp.where(low, swapped, -swapped)], axis=0).T
    left = turn[pl.ds(pl.multiple_of(pix * count, count), count), :]
    right = jnp.concatenate([edge, edge], axis=0).astype(BF16)
    lane = lax.broadcasted_iota(jnp.int32, left.shape, 1)
    for part in range(2):
        got = got_ref[part * count : (part + 1) * count, :].astype(F32)
        chosen = jnp.where((lane < 8) if part == 0 else (lane >= 8), left, 0.0).astype(BF16)
        update = jnp.dot(chosen, right, preferred_element_type=F32)
        vis_ref[0, part] = (rows_ref[part] + got + update) * inv_total
    own_power = jnp.sum(jnp.sum(edge * edge, axis=1, keepdims=True), axis=0, keepdims=True)
    for q in range(groups):
        got = got_ref[2 * count + at + 8 + q : 2 * count + at + 9 + q, :].astype(F32)
        beams = extra_ref[8 * q : 8 * q + 8, :] + got_ref[
            2 * count + 8 * q : 2 * count + 8 * q + 8, :
        ].astype(F32)
        power = jnp.sum(beams * beams, axis=0, keepdims=True) - own_power
        image_ref[:, q * STATIONS : (q + 1) * STATIONS] = (
            extra_ref[at + 8 + q : at + 9 + q, :] + got + power
        ) * (inv_total * image_scale)


def finish(rows, extra, got, pixels, inv_total, image_scale):
    count = rows.shape[1]
    return pl.pallas_call(
        lambda *refs: finish_kernel(inv_total, image_scale, *refs),
        out_shape=(
            jax.ShapeDtypeStruct((1, 2, count, STATIONS), F32),
            jax.ShapeDtypeStruct((1, pixels), F32),
        ),
        in_specs=[VMEM] * 3,
        out_specs=(VMEM, VMEM),
        scratch_shapes=[pltpu.VMEM((STATIONS, 16), F32)],
        name="finish",
        **params(1 << 20, 1 << 18),
    )(rows, extra, got)


def on_device(voltages, fir_taps, station_of_slot, station_u, station_v, pixel_l, pixel_m):
    spec_dev = voltages.shape[1]
    pix_count = lax.axis_size("pix")
    spectra_total = spec_dev * pix_count
    pix = lax.axis_index("pix")
    across = jnp.where(pix < 2, pix + 2, pix - 2)
    rows_l = pixel_l.shape[0] // pix_count
    sent = filter_bank(voltages, fir_taps).reshape(POINTS, ROWS // 2, 2, LANES)
    received = lax.all_to_all(
        sent, "chan", split_axis=0, concat_axis=0, tiled=True, axis_index_groups=[BACKWARDS]
    )

    block_l = jnp.concatenate(
        [
            lax.dynamic_slice_in_dim(pixel_l, pix * rows_l, rows_l, 0),
            lax.dynamic_slice_in_dim(pixel_l, across * rows_l, rows_l, 0),
            jnp.zeros((LANES - 2 * rows_l,), jnp.int32),
        ]
    )[None]
    pixels = rows_l * pixel_m.shape[0]
    here_cos, here_sin, across_cos, across_sin = steering(
        lax.axis_index("chan")[None].astype(jnp.int32),
        station_u[None],
        station_v[None],
        block_l,
        jnp.concatenate([pixel_m, pixel_m])[None],
        pixels,
    )
    station_row = station_of_slot.reshape(POINTS, 2)[::-1].T.reshape(1, STATIONS)
    own = gram(received.reshape(-1, LANES), station_row, here_cos)
    other = lax.ppermute(own, "pix", [(0, 1), (1, 0), (2, 3), (3, 2)])
    count = STATIONS // pix_count
    send = send_part(own, other, across_cos, across_sin, count)
    got = lax.ppermute(send, "pix", [(0, 2), (2, 0), (1, 3), (3, 1)])
    rows, extra = keep_part(own, other, here_cos, here_sin, send, count)
    return finish(rows, extra, got, pixels, 1.0 / spectra_total, math.sqrt(spectra_total) / STATIONS)


def solution(mesh):
    in_specs = (P("chan", "pix", None), P(), P(), P(), P(), P(), P())
    out_specs = (P("chan", None, "pix", None), P("chan", "pix"))
    return jax.shard_map(
        on_device, mesh=mesh, in_specs=in_specs, out_specs=out_specs, check_vma=False
    )
```
